512 devices in a mesh: seq: 128 (over y, z, core), head: 4 (over x).
Axes of the slice: x: 4, y: 8, z: 8, core: 2. Of those that a mesh axis runs over, the one named last changes fastest.
Arguments:
- queries_first: bfloat16 [65536, 1024], P('seq', 'head'), may hold values from -4.4 to 4.4
- keys_first: bfloat16 [65536, 1024], P('seq', 'head'), may hold values from -4.4 to 4.4
- values_first: bfloat16 [65536, 1024], P('seq', 'head'), may hold values from -6 to 6
- input_map: bfloat16 [4, 256, 512], P('head'), may hold values from -0.375 to 0.375
- fast_keys: bfloat16 [65536, 2048], P('seq', 'head'), may hold values from -6 to 6
- fast_values: bfloat16 [65536, 2048], P('seq', 'head'), may hold values from -24 to 24
- step_rates: float32 [65536, 4], P('seq', 'head'), may hold values from 0.1 to 1
- fast_weights: bfloat16 [4, 512, 3, 512], P('head'), may hold values from -6 to 6
- output_map: bfloat16 [2048, 1024], P('head'), may hold values from -0.25 to 0.25
- queries_second: bfloat16 [65536, 1024], P('seq', 'head'), may hold values from -4.4 to 4.4
- keys_second: bfloat16 [65536, 1024], P('seq', 'head'), may hold values from -4.4 to 4.4
- values_second: bfloat16 [65536, 1024], P('seq', 'head'), may hold values from -6 to 6
Outputs:
- block_output: bfloat16 [65536, 1024], P('seq', 'head')
- new_weights: bfloat16 [4, 512, 3, 512], P('head', 'seq')
The draws below stay inside these ranges and needn't reach their ends.
All inputs are finite; a program needn't handle non-finite values.
Results may differ from the reference program's by a relative error of at most 0.034.
Values may be sent and summed in bfloat16 or wider, within the bound.
A program may use at most 64 MiB of HBM per device.

```python
import math
import jax
import jax.numpy as jnp
from jax import lax

HALF_WIN = 512
HEAD_DIM = 128
HEADS_GRP = 2
FAST_DIM = 512
FAST_HIDDEN = 512
GROUPS = 4
TOKENS = 65536


def qk_pair(key, salt):
    base = jax.random.fold_in(key, salt)
    key_query, key_keys = jax.random.split(base, 2)
    array_shape = (TOKENS, GROUPS * HEADS_GRP * HEAD_DIM)
    queries = jnp.clip(jax.random.normal(key_query, array_shape, jnp.float32), -4.375, 4.375)
    key_rows = jnp.clip(jax.random.normal(key_keys, array_shape, jnp.float32), -4.375, 4.375)
    return (queries, key_rows)


def draw_queries_first(key, part):
    return qk_pair(key, 11)[0].astype(jnp.bfloat16)


def draw_keys_first(key, part):
    return qk_pair(key, 11)[1].astype(jnp.bfloat16)


def draw_queries_second(key, part):
    return qk_pair(key, 23)[0].astype(jnp.bfloat16)


def draw_keys_second(key, part):
    return qk_pair(key, 23)[1].astype(jnp.bfloat16)


def draw_fast_weights(key, part):
    base = jax.random.fold_in(key, 37)
    key_rows, key_cols, key_main = jax.random.split(base, 3)
    array_shape = (GROUPS, FAST_HIDDEN, 3, FAST_DIM)
    row_scale = jnp.exp(jax.random.uniform(key_rows, (GROUPS, FAST_HIDDEN, 3, 1), jnp.float32) * 2.302585) / 3.16
    col_scale = jnp.exp(jax.random.uniform(key_cols, (GROUPS, 1, 3, FAST_DIM), jnp.float32) * 2.302585) / 4.64
    entries = jnp.clip(jax.random.normal(key_main, array_shape, jnp.float32), -4.0, 4.0)
    return jnp.clip(entries * row_scale * col_scale, -6.0, 6.0).astype(jnp.bfloat16)


def raised(array, rng, source, target, blocks, factor):
    owner, partner = [(jnp.arange(array.shape[dim]) // (array.shape[dim] // blocks)).reshape([-1 if axis == dim else 1 for axis in range(array.ndim)]) for dim in (source, target)]
    chosen = jax.random.permutation(rng, blocks)[partner]
    strong = (owner == chosen) | (owner == (partner + blocks // 2) % blocks)
    return jnp.where(strong, factor * array, array)


def steps_of(own_key, extent, shards, smallest, largest):
    def one(position, blocks):
        heights = jax.random.uniform(jax.random.fold_in(jax.random.fold_in(own_key, 6), position), (blocks,), jnp.float32, smallest / len(shards), largest / len(shards))
        return jnp.repeat(jnp.exp(heights), extent[position] // blocks).reshape((-1,) + (1,) * (len(extent) - position - 1))

    level = one(*shards[0])
    for cut in shards[1:]:
        level = level * one(*cut)
    return level


def noise(own_key, shape, spread, most, cuts=(), kind=jnp.bfloat16):
    level = steps_of(own_key, shape, cuts, -0.22, 0.18) if cuts else 1.0
    array = jax.random.normal(own_key, shape, jnp.float32) * spread * level
    return jnp.minimum(jnp.maximum(array, -most), most).astype(kind)


def gaussian_with(own_key, extent, width, reach, pieces, heavy, kind=jnp.bfloat16):
    values = width * jax.random.normal(own_key, extent, jnp.float32)
    if pieces:
        values = values * steps_of(own_key, extent, pieces, -0.22, 0.18)
    return jnp.clip(raised(values, jax.random.fold_in(own_key, 3), *heavy), -reach, reach).astype(kind)


def setup_inputs(seed: int = 0) -> dict:
    streams_of = jax.random.split(jax.random.key(seed), 13)
    queries_first = draw_queries_first(jax.random.fold_in(streams_of[12], 71), 0)
    keys_first = draw_keys_first(jax.random.fold_in(streams_of[12], 71), 0)
    values_first = noise(streams_of[2], (TOKENS, GROUPS * HEADS_GRP * HEAD_DIM), 1.0, 6.0, ((0, 128), (1, 4)))
    input_map = noise(streams_of[3], (GROUPS, HEADS_GRP * HEAD_DIM, FAST_DIM), (HEADS_GRP * HEAD_DIM) ** -0.5, 0.375, ((0, 4),))
    fast_keys = noise(streams_of[4], (TOKENS, GROUPS * FAST_DIM), 1.0, 6.0, ((0, 128), (1, 4)))
    fast_values = gaussian_with(streams_of[5], (TOKENS, GROUPS * FAST_DIM), 1.0, 24.0, ((0, 128), (1, 4)), (0, 1, 128, 5.5))
    step_rates = jnp.clip(jnp.exp(math.log(1.0) - 2.3025851 * jax.random.uniform(streams_of[6], (TOKENS, GROUPS), jnp.float32) ** steps_of(streams_of[6], (TOKENS, GROUPS), ((0, 128), (1, 4)), -0.2, 0.2)), 0.1, 1.0)
    fast_weights = draw_fast_weights(jax.random.fold_in(streams_of[12], 71), 0)
    output_map = noise(streams_of[8], (GROUPS * FAST_DIM, GROUPS * HEADS_GRP * HEAD_DIM), FAST_DIM ** -0.5, 0.25, ((0, 4),))
    queries_second = draw_queries_second(jax.random.fold_in(streams_of[12], 71), 0)
    keys_second = draw_keys_second(jax.random.fold_in(streams_of[12], 71), 0)
    values_second = noise(streams_of[11], (TOKENS, GROUPS * HEADS_GRP * HEAD_DIM), 1.0, 6.0, ((0, 128), (1, 4)))
    return dict(queries_first=queries_first, keys_first=keys_first, values_first=values_first, input_map=input_map, fast_keys=fast_keys, fast_values=fast_values, step_rates=step_rates, fast_weights=fast_weights, output_map=output_map, queries_second=queries_second, keys_second=keys_second, values_second=values_second)


def rms_round(matrix):
    return (matrix * lax.rsqrt(lax.optimization_barrier(jnp.mean(matrix * matrix, axis=-1, keepdims=True)) + 1e-05)).astype(jnp.bfloat16)

def window_attend(queries, key_rows, value_rows):
    block_rows = min(512, TOKENS)
    span_rows = block_rows + 2 * HALF_WIN
    keys_ext = jnp.pad(key_rows, ((HALF_WIN, HALF_WIN), (0, 0)))
    values_ext = jnp.pad(value_rows, ((HALF_WIN, HALF_WIN), (0, 0)))
    inverse_root = 1.0 / math.sqrt(HEAD_DIM)

    def attend_block(block_index):
        start_row = (block_index * block_rows).astype(jnp.int32)
        query_block = lax.dynamic_slice_in_dim(queries, start_row, block_rows, 0).reshape(block_rows, HEADS_GRP, HEAD_DIM)
        key_block = lax.dynamic_slice_in_dim(keys_ext, start_row, span_rows, 0).reshape(span_rows, HEADS_GRP, HEAD_DIM)
        value_block = lax.dynamic_slice_in_dim(values_ext, start_row, span_rows, 0).reshape(span_rows, HEADS_GRP, HEAD_DIM)
        scores = jnp.einsum('qhd,khd->hqk', query_block.astype(jnp.float32), key_block.astype(jnp.float32)) * inverse_root
        query_pos = jnp.arange(block_rows, dtype=jnp.int32)[:, None]
        key_pos = jnp.arange(span_rows, dtype=jnp.int32)[None, :]
        global_pos = start_row + key_pos - HALF_WIN
        allowed = (key_pos >= query_pos) & (key_pos <= query_pos + 2 * HALF_WIN) & (global_pos >= 0) & (global_pos < TOKENS)
        scores = jnp.where(allowed[None], scores, -jnp.inf)
        highest = lax.optimization_barrier(jnp.max(scores, axis=-1, keepdims=True))
        weights_exp = jnp.exp(scores - highest)
        weights_bf = (weights_exp / lax.optimization_barrier(jnp.sum(weights_exp, axis=-1, keepdims=True))).astype(jnp.bfloat16)
        attended = jnp.einsum('hqk,khd->qhd', weights_bf.astype(jnp.float32), value_block.astype(jnp.float32))
        return rms_round(attended.reshape(block_rows, HEADS_GRP * HEAD_DIM))
    outputs = lax.map(attend_block, jnp.arange(TOKENS // block_rows, dtype=jnp.int32))
    return outputs.reshape(TOKENS, HEADS_GRP * HEAD_DIM)

def swiglu_apply(fast_query, weights_rows):
    inverse = 1.0 / math.sqrt(FAST_DIM)
    gate_part = jnp.dot(fast_query, weights_rows[:, 0, :].T, preferred_element_type=jnp.float32) * inverse
    up_part = jnp.dot(fast_query, weights_rows[:, 1, :].T, preferred_element_type=jnp.float32) * inverse
    hidden_query = (jax.nn.silu(gate_part) * up_part).astype(jnp.bfloat16)
    return jnp.dot(hidden_query, weights_rows[:, 2, :], preferred_element_type=jnp.float32)

def renormalize(old_rows, gradient_rows, factor):
    old_float = old_rows.astype(jnp.float32)
    stepped = old_float + factor * gradient_rows
    old_norm = jnp.sqrt(lax.optimization_barrier(jnp.sum(old_float * old_float, axis=-1, keepdims=True)))
    return (stepped * old_norm * lax.rsqrt(lax.optimization_barrier(jnp.sum(stepped * stepped, axis=-1, keepdims=True)) + 1e-06)).astype(jnp.bfloat16)

def reference(queries_first, keys_first, values_first, input_map, fast_keys, fast_values, step_rates, fast_weights, output_map, queries_second, keys_second, values_second):
    group_width = HEADS_GRP * HEAD_DIM
    inverse = 1.0 / math.sqrt(FAST_DIM)
    limit_norm = math.sqrt(FAST_HIDDEN * FAST_DIM) / 2.0
    fast_list = []
    weight_list = []
    for group in range(GROUPS):
        low_col = group * group_width
        normed_first = window_attend(queries_first[:, low_col:low_col + group_width], keys_first[:, low_col:low_col + group_width], values_first[:, low_col:low_col + group_width])
        fast_query = jnp.dot(normed_first, input_map[group], preferred_element_type=jnp.float32).astype(jnp.bfloat16)
        weights_local = fast_weights[group]
        keys_fast = fast_keys[:, group * FAST_DIM:(group + 1) * FAST_DIM]
        values_fast = fast_values[:, group * FAST_DIM:(group + 1) * FAST_DIM]
        rates_col = step_rates[:, group:group + 1]
        gate_keys = jnp.dot(keys_fast, weights_local[:, 0, :].T, preferred_element_type=jnp.float32) * inverse
        up_keys = jnp.dot(keys_fast, weights_local[:, 1, :].T, preferred_element_type=jnp.float32) * inverse
        sigmoid_gate = jax.nn.sigmoid(gate_keys)
        silu_gate = gate_keys * sigmoid_gate
        hidden_keys = (rates_col * silu_gate * up_keys).astype(jnp.bfloat16)
        backward = rates_col * jnp.dot(values_fast, weights_local[:, 2, :].T, preferred_element_type=jnp.float32)
        d_gate = (backward * up_keys * sigmoid_gate * (1.0 + gate_keys * (1.0 - sigmoid_gate)) * inverse).astype(jnp.bfloat16)
        d_up = (backward * silu_gate * inverse).astype(jnp.bfloat16)
        gradient = jnp.stack([jnp.dot(d_gate.T, keys_fast, preferred_element_type=jnp.float32), jnp.dot(d_up.T, keys_fast, preferred_element_type=jnp.float32), jnp.dot(hidden_keys.T, values_fast, preferred_element_type=jnp.float32)], axis=1)
        factor = jnp.minimum(1.0, limit_norm * lax.rsqrt(jnp.sum(gradient * gradient) + 1e-06))
        updated = renormalize(weights_local, gradient, factor)
        fast_list.append(rms_round(swiglu_apply(fast_query, updated)))
        weight_list.append(updated)
    mixed = jnp.zeros((TOKENS, GROUPS * group_width), jnp.float32)
    for group in range(GROUPS):
        product = jnp.dot(fast_list[group], output_map[group * FAST_DIM:(group + 1) * FAST_DIM], preferred_element_type=jnp.float32)
        mixed = mixed + lax.optimization_barrier(product.astype(jnp.bfloat16)).astype(jnp.float32)
    query_two = (queries_second.astype(jnp.float32) + mixed).astype(jnp.bfloat16)
    out_list = []
    for group in range(GROUPS):
        low_col = group * group_width
        out_list.append(window_attend(query_two[:, low_col:low_col + group_width], keys_second[:, low_col:low_col + group_width], values_second[:, low_col:low_col + group_width]))
    return (jnp.concatenate(out_list, axis=1), jnp.stack(weight_list))
```

```python
import math

import jax
import jax.numpy as jnp
from jax import lax
from jax.experimental import pallas as pl
from jax.experimental.pallas import tpu as pltpu
from jax.sharding import PartitionSpec as P

MESH = pl.DeviceIdType.MESH
BF = jnp.bfloat16
F32 = jnp.float32
WIN = 512
HD = 128
GW = 256
FD = 512
RING = 8
HALF = 768
PIECE = HALF // RING
SCALE2 = math.log2(math.e) / math.sqrt(HD)
INV = 1.0 / math.sqrt(FD)
LIMIT = math.sqrt(FD * FD) / 2.0
ORDER = (4, 3, 5, 2, 6, 1, 7)
NT = (((1,), (1,)), ((), ()))


def remote(src, dst, send, recv, peer):
    return pltpu.make_async_remote_copy(
        src_ref=src, dst_ref=dst, send_sem=send, recv_sem=recv, device_id=peer, device_id_type=MESH
    )


def rows(start, size):
    return pl.ds(pl.multiple_of(start, size), size)


def attend(query, kext, vext, out, start, count, first, last):
    span = count + 2 * WIN
    before, after = WIN - start, WIN + WIN - start
    row = lax.broadcasted_iota(jnp.int32, (count, 1), 0)
    low = jnp.maximum(row, jnp.where(first, before, 0))
    high = jnp.minimum(row + 2 * WIN, jnp.where(last, after - 1, span))
    col_b = lax.broadcasted_iota(jnp.int32, (count, before), 1)
    col_a = lax.broadcasted_iota(jnp.int32, (count, span - after), 1) + after
    keep_b, keep_a = col_b >= low, col_a <= high
    parts = []
    for head in range(GW // HD):
        lanes = slice(head * HD, (head + 1) * HD)
        scores = lax.dot_general(
            query[:, lanes], kext[start : start + span, lanes], NT, preferred_element_type=F32
        )
        s_b = jnp.where(keep_b, scores[:, :before], -jnp.inf)
        s_o = scores[:, before:after]
        s_a = jnp.where(keep_a, scores[:, after:], -jnp.inf)
        top = jnp.maximum(
            jnp.max(s_o, axis=1, keepdims=True),
            jnp.maximum(jnp.max(s_b, axis=1, keepdims=True), jnp.max(s_a, axis=1, keepdims=True)),
        )
        shift = top * SCALE2
        e_b, e_o, e_a = (jnp.exp2(s * SCALE2 - shift) for s in (s_b, s_o, s_a))
        total = (
            jnp.sum(e_b, axis=1, keepdims=True)
            + jnp.sum(e_o, axis=1, keepdims=True)
            + jnp.sum(e_a, axis=1, keepdims=True)
        )
        probs = jnp.concatenate([e_b.astype(BF), e_o.astype(BF), e_a.astype(BF)], axis=1)
        mixed = jnp.dot(probs, vext[start : start + span, lanes], preferred_element_type=F32)
        parts.append(mixed / total)
    square = sum(jnp.sum(p * p, axis=1, keepdims=True) for p in parts)
    norm = lax.rsqrt(square * (1.0 / GW) + 1e-05)
    for head, part in enumerate(parts):
        out[:, head * HD : (head + 1) * HD] = (part * norm).astype(BF)


def update_kernel(
    q_in, k_in, v_in, map_in, fk_in, fv_in, rates, w_in,
    w_out, fq_out,
    fk, fv, w, q, fmap, kext, vext, normed, part_out, part_in, own, mine, got1, sum1, got2, full, halves,
    load_sem, halo_send, halo_recv, pair_send, pair_recv, s1, r1, s2, r2, s3, r3, s4, r4, s5, r5,
):
    seq, head = lax.axis_index("seq"), lax.axis_index("head")
    n_seq = lax.axis_size("seq")
    core = lax.rem(seq, 2)
    y, z = seq // (2 * RING), lax.rem(seq // 2, RING)
    pos1 = jnp.where(core == 0, y, z)
    pos2 = jnp.where(core == 0, z, y)
    other1 = pos2
    stride1 = jnp.where(core == 0, 2 * RING, 2)
    stride2 = jnp.where(core == 0, 2, 2 * RING)

    def ring1(place):
        return (seq + (place - pos1) * stride1, head)

    def ring2(place):
        return (seq + (place - pos2) * stride2, head)

    def ahead(position, step):
        return lax.rem(position + step, RING)

    partner = (seq + 1 - 2 * core, head)
    following = (lax.rem(seq + 1, n_seq), head)
    previous = (lax.rem(seq + n_seq - 1, n_seq), head)
    outer = (jnp.where(core == 0, previous[0], following[0]), head)

    loads = [
        pltpu.make_async_copy(w_in, w, load_sem.at[0]),
        pltpu.make_async_copy(fk_in, fk, load_sem.at[1]),
        pltpu.make_async_copy(fv_in, fv, load_sem.at[2]),
        pltpu.make_async_copy(k_in, kext.at[WIN : 2 * WIN], load_sem.at[3]),
        pltpu.make_async_copy(v_in, vext.at[WIN : 2 * WIN], load_sem.at[4]),
        pltpu.make_async_copy(q_in, q, load_sem.at[5]),
        pltpu.make_async_copy(map_in, fmap, load_sem.at[6]),
    ]
    for copy in loads:
        copy.start()

    barrier = pltpu.get_barrier_semaphore()
    for step in range(1, RING):
        pl.semaphore_signal(barrier, inc=1, device_id=ring1(ahead(pos1, step)), device_id_type=MESH)
        pl.semaphore_signal(barrier, inc=1, device_id=ring2(ahead(pos2, step)), device_id_type=MESH)
    pl.semaphore_signal(barrier, inc=1, device_id=partner, device_id_type=MESH)
    pl.semaphore_signal(barrier, inc=1, device_id=outer, device_id_type=MESH)

    for copy in loads[:3]:
        copy.wait()

    def gradient_half(which, emit):
        block = rows(which * GW, GW)
        keys, values = fk[...], fv[...]
        gate = lax.dot_general(w[0, block, :], keys, NT, preferred_element_type=F32) * INV
        up = lax.dot_general(w[1, block, :], keys, NT, preferred_element_type=F32) * INV
        rate = rates[...]
        backward = rate * lax.dot_general(w[2, block, :], values, NT, preferred_element_type=F32)
        sigmoid = 1.0 / (1.0 + jnp.exp(-gate))
        silu = gate * sigmoid
        hidden = (rate * silu * up).astype(BF)
        d_gate = (backward * up * sigmoid * (1.0 + gate * (1.0 - sigmoid)) * INV).astype(BF)
        d_up = (backward * silu * INV).astype(BF)
        emit(0, jnp.dot(d_gate, keys, preferred_element_type=F32))
        emit(1, jnp.dot(d_up, keys, preferred_element_type=F32))
        emit(2, jnp.dot(hidden, values, preferred_element_type=F32))

    pl.semaphore_wait(barrier, 2 * (RING - 1) + 2)
    halo = [
        remote(k_in, kext.at[0:WIN], halo_send.at[0], halo_recv.at[0], following),
        remote(v_in, vext.at[0:WIN], halo_send.at[1], halo_recv.at[1], following),
        remote(k_in, kext.at[2 * WIN :], halo_send.at[2], halo_recv.at[2], previous),
        remote(v_in, vext.at[2 * WIN :], halo_send.at[3], halo_recv.at[3], previous),
    ]
    for copy in halo:
        copy.start()

    pair = [
        remote(part_out.at[m], part_in.at[m], pair_send.at[m], pair_recv.at[m], partner)
        for m in range(3)
    ]

    def emit_partner(m, value):
        part_out[m] = value.astype(BF)
        pair[m].start()

    def emit_own(m, value):
        own[m * GW : (m + 1) * GW] = value

    gradient_half(1 - core, emit_partner)
    gradient_half(core, emit_own)

    for m in range(3):
        pair[m].wait_recv()
        block = slice(m * GW, (m + 1) * GW)
        total = own[block] + part_in[m].astype(F32)
        own[block] = total
        mine[block] = total.astype(BF)

    first_stage = {
        step: remote(
            mine.at[rows(ahead(pos1, step) * PIECE, PIECE)],
            got1.at[step - 1],
            s1.at[step - 1],
            r1.at[step - 1],
            ring1(ahead(pos1, step)),
        )
        for step in ORDER
    }
    for step in ORDER:
        first_stage[step].start()

    for copy in loads[3:]:
        copy.wait()
    for copy in halo:
        copy.wait_recv()
    first, last = seq == 0, seq == n_seq - 1
    for start in (0, GW):
        block = slice(start, start + GW)
        attend(q.at[block], kext, vext, normed.at[block], start, GW, first, last)
    fq_out[...] = jnp.dot(normed[...], fmap[...], preferred_element_type=F32).astype(BF)

    for step in ORDER:
        first_stage[step].wait_recv()
    total = own[rows(pos1 * PIECE, PIECE)]
    for step in range(1, RING):
        total = total + got1[step - 1].astype(F32)
    sum1[0] = total.astype(BF)
    halves[...] = total

    def quarter(place):
        return (rows((place // 4) * (PIECE // 2), PIECE // 2), rows(lax.rem(place, 4) * HD, HD))

    second_stage = {
        step: remote(
            sum1.at[0].at[quarter(ahead(pos2, step))],
            got2.at[step - 1],
            s2.at[step - 1],
            r2.at[step - 1],
            ring2(ahead(pos2, step)),
        )
        for step in ORDER
    }
    for step in ORDER:
        second_stage[step].start()
    for step in ORDER:
        second_stage[step].wait_recv()
    total = halves[quarter(pos2)]
    for step in range(1, RING):
        total = total + got2[step - 1].astype(F32)
    here = full.at[core].at[rows(pos1 * PIECE, PIECE)]
    here.at[quarter(pos2)][...] = total.astype(BF)

    third_stage = {
        step: remote(
            here.at[quarter(pos2)],
            here.at[quarter(pos2)],
            s3.at[step - 1],
            r3.at[step - 1],
            ring2(ahead(pos2, step)),
        )
        for step in ORDER
    }
    for step in ORDER:
        third_stage[step].start()
    for step in ORDER:
        third_stage[step].wait_recv()

    fourth_stage = {
        step: remote(here, here, s4.at[step - 1], r4.at[step - 1], ring1(ahead(pos1, step)))
        for step in ORDER
    }
    for step in ORDER:
        fourth_stage[step].start()

    def across(step):
        block = full.at[core].at[rows(ahead(pos1, RING - step) * PIECE, PIECE)]
        return remote(block, block, s5.at[step], r5.at[step], partner)

    across(0).start()
    for step in (1, 7, 2, 6, 3, 5, 4):
        fourth_stage[step].wait_recv()
        across(step).start()
    for step in range(RING):
        block = full.at[1 - core].at[rows(ahead(other1, RING - step) * PIECE, PIECE)]
        remote(block, block, s5.at[step], r5.at[step], partner).wait_recv()

    def squares(i, acc):
        block = full[i // 12, rows(lax.rem(i, 12) * 64, 64), :].astype(F32)
        return acc + jnp.sum(block * block, axis=0, keepdims=True)

    acc = lax.fori_loop(0, 24, squares, jnp.zeros((1, FD), F32))
    energy = jnp.sum(acc, axis=1, keepdims=True)
    factor = jnp.minimum(1.0, LIMIT * lax.rsqrt(energy + 1e-06))

    def renew(i, carry):
        m, r = i // 8, lax.rem(i, 8)
        old = w[m, rows(r * 64, 64), :].astype(F32)
        grad = full[r // 4, rows(m * GW + lax.rem(r, 4) * 64, 64), :].astype(F32)
        stepped = old + factor * grad
        norm = jnp.sqrt(jnp.sum(old * old, axis=1, keepdims=True))
        scale = norm * lax.rsqrt(jnp.sum(stepped * stepped, axis=1, keepdims=True) + 1e-06)
        w_out[m, rows(r * 64, 64), :] = (stepped * scale).astype(BF)
        return carry

    lax.fori_loop(0, 24, renew, 0)

    for copy in halo:
        copy.wait_send()
    for copy in pair:
        copy.wait_send()
    for step in ORDER:
        first_stage[step].wait_send()
        second_stage[step].wait_send()
        third_stage[step].wait_send()
        fourth_stage[step].wait_send()
    for step in range(RING):
        across(step).wait_send()


def query_kernel(
    fq, w, map_in, q_in, k_in, v_in,
    out,
    omap, q, kext, vext, product, direct, relay, joined_out, joined, two,
    load_sem, halo_send, halo_recv, ds, dr, rs, rr, js, jr,
):
    seq, head = lax.axis_index("seq"), lax.axis_index("head")
    n_seq, n_head = lax.axis_size("seq"), lax.axis_size("head")
    core = lax.rem(seq, 2)
    following = (lax.rem(seq + 1, n_seq), head)
    previous = (lax.rem(seq + n_seq - 1, n_seq), head)
    toward = jnp.where(core == 0, 1, n_head - 1)
    near = lax.rem(head + toward, n_head)
    back = lax.rem(head + n_head - toward, n_head)
    far = lax.rem(head + 2, n_head)

    loads = [
        pltpu.make_async_copy(map_in, omap, load_sem.at[0]),
        pltpu.make_async_copy(q_in, q, load_sem.at[1]),
        pltpu.make_async_copy(k_in, kext.at[WIN : 2 * WIN], load_sem.at[2]),
        pltpu.make_async_copy(v_in, vext.at[WIN : 2 * WIN], load_sem.at[3]),
    ]
    for copy in loads:
        copy.start()
    barrier = pltpu.get_barrier_semaphore()
    for peer in ((seq, near), (seq, back), following, previous):
        pl.semaphore_signal(barrier, inc=1, device_id=peer, device_id_type=MESH)

    chunks = 4
    size = WIN // chunks
    halo = [
        remote(k_in, kext.at[0:WIN], halo_send.at[0], halo_recv.at[0], following),
        remote(v_in, vext.at[0:WIN], halo_send.at[1], halo_recv.at[1], following),
        remote(k_in, kext.at[2 * WIN :], halo_send.at[2], halo_recv.at[2], previous),
        remote(v_in, vext.at[2 * WIN :], halo_send.at[3], halo_recv.at[3], previous),
    ]

    def columns(group):
        return rows(group * GW, GW)

    def to_relay(i):
        block = slice(i * size, (i + 1) * size)
        return remote(
            product.at[block, columns(far)], relay.at[i], rs.at[i], rr.at[i], (seq, near)
        )

    def to_back(i):
        block = slice(i * size, (i + 1) * size)
        return remote(
            product.at[block, columns(back)], direct.at[i], ds.at[i], dr.at[i], (seq, back)
        )

    def to_near(i):
        return remote(joined_out.at[i], joined.at[i], js.at[i], jr.at[i], (seq, near))

    def join(i):
        to_relay(i).wait_recv()
        block = slice(i * size, (i + 1) * size)
        value = product[block, columns(near)].astype(F32) + relay[i].astype(F32)
        joined_out[i] = value.astype(BF)
        to_near(i).start()

    for i in range(chunks):
        block = slice(i * size, (i + 1) * size)
        query = fq[block]
        gate = lax.dot_general(query, w[0], NT, preferred_element_type=F32) * INV
        up = lax.dot_general(query, w[1], NT, preferred_element_type=F32) * INV
        hidden = (gate / (1.0 + jnp.exp(-gate)) * up).astype(BF)
        raw = jnp.dot(hidden, w[2], preferred_element_type=F32)
        mean = jnp.sum(raw * raw, axis=1, keepdims=True) * (1.0 / FD)
        fast = (raw * lax.rsqrt(mean + 1e-05)).astype(BF)
        if i == 0:
            loads[0].wait()
        product[block] = jnp.dot(fast, omap[...], preferred_element_type=F32).astype(BF)
        if i == 0:
            pl.semaphore_wait(barrier, 4)
        to_relay(i).start()
        to_back(i).start()
        if i == 0:
            for copy in halo:
                copy.start()
        if i > 0:
            join(i - 1)
    join(chunks - 1)

    for copy in loads[1:]:
        copy.wait()
    for copy in halo:
        copy.wait_recv()
    first, last = seq == 0, seq == n_seq - 1
    for start in (0, GW):
        for i in range(start // size, (start + GW) // size):
            block = slice(i * size, (i + 1) * size)
            to_back(i).wait_recv()
            to_near(i).wait_recv()
            mixed = (
                product[block, columns(head)].astype(F32)
                + direct[i].astype(F32)
                + joined[i].astype(F32)
            )
            two[block] = (q[block].astype(F32) + mixed).astype(BF)
        block = slice(start, start + GW)
        attend(two.at[block], kext, vext, out.at[block], start, GW, first, last)

    for copy in halo:
        copy.wait_send()
    for i in range(chunks):
        to_relay(i).wait_send()
        to_back(i).wait_send()
        to_near(i).wait_send()


def local(
    queries_first,
    keys_first,
    values_first,
    input_map,
    fast_keys,
    fast_values,
    step_rates,
    fast_weights,
    output_map,
    queries_second,
    keys_second,
    values_second,
):
    anywhere = pl.BlockSpec(memory_space=pltpu.HBM)
    vmem = pl.BlockSpec(memory_space=pltpu.VMEM)
    dma = pltpu.SemaphoreType.DMA
    seq = lax.axis_index("seq")
    weights = jnp.transpose(fast_weights[0], (1, 0, 2))
    new_weights, fast_query = pl.pallas_call(
        update_kernel,
        out_shape=(
            jax.ShapeDtypeStruct((3, FD, FD), BF),
            jax.ShapeDtypeStruct((WIN, FD), BF),
        ),
        in_specs=[anywhere] * 6 + [vmem, anywhere],
        out_specs=(vmem, vmem),
        scratch_shapes=[
            pltpu.VMEM((WIN, FD), BF),
            pltpu.VMEM((WIN, FD), BF),
            pltpu.VMEM((3, FD, FD), BF),
            pltpu.VMEM((WIN, GW), BF),
            pltpu.VMEM((GW, FD), BF),
            pltpu.VMEM((3 * WIN, GW), BF),
            pltpu.VMEM((3 * WIN, GW), BF),
            pltpu.VMEM((WIN, GW), BF),
            pltpu.VMEM((3, GW, FD), BF),
            pltpu.VMEM((3, GW, FD), BF),
            pltpu.VMEM((HALF, FD), F32),
            pltpu.VMEM((HALF, FD), BF),
            pltpu.VMEM((RING - 1, PIECE, FD), BF),
            pltpu.VMEM((1, PIECE, FD), BF),
            pltpu.VMEM((RING - 1, PIECE // 2, HD), BF),
            pltpu.VMEM((2, HALF, FD), BF),
            pltpu.VMEM((PIECE, FD), F32),
            dma((7,)),
            dma((4,)),
            dma((4,)),
            dma((3,)),
            dma((3,)),
        ]
        + [dma((RING,))] * 10,
        compiler_params=pltpu.CompilerParams(
            collective_id=0, has_side_effects=True, vmem_limit_bytes=66_900_000
        ),
        name="update",
    )(
        queries_first,
        keys_first,
        values_first,
        input_map[0],
        fast_keys,
        fast_values,
        step_rates.reshape(1, WIN),
        weights,
    )
    share = FD // lax.axis_size("seq")
    own_new = lax.dynamic_slice_in_dim(jnp.transpose(new_weights, (1, 0, 2)), seq * share, share, 0)
    quarter = WIN // 4
    block_output = pl.pallas_call(
        query_kernel,
        out_shape=jax.ShapeDtypeStruct((WIN, GW), BF),
        in_specs=[vmem, vmem] + [anywhere] * 4,
        out_specs=vmem,
        scratch_shapes=[
            pltpu.VMEM((FD, 4 * GW), BF),
            pltpu.VMEM((WIN, GW), BF),
            pltpu.VMEM((3 * WIN, GW), BF),
            pltpu.VMEM((3 * WIN, GW), BF),
            pltpu.VMEM((WIN, 4 * GW), BF),
            pltpu.VMEM((4, quarter, GW), BF),
            pltpu.VMEM((4, quarter, GW), BF),
            pltpu.VMEM((4, quarter, GW), BF),
            pltpu.VMEM((4, quarter, GW), BF),
            pltpu.VMEM((WIN, GW), BF),
            dma((4,)),
            dma((4,)),
            dma((4,)),
        ]
        + [dma((4,))] * 6,
        compiler_params=pltpu.CompilerParams(
            collective_id=1, has_side_effects=True, vmem_limit_bytes=66_900_000
        ),
        name="query",
    )(fast_query, new_weights, output_map, queries_second, keys_second, values_second)
    return (block_output, own_new[None])


def solution(mesh):
    return jax.shard_map(
        local,
        mesh=mesh,
        in_specs=(
            P("seq", "head"),
            P("seq", "head"),
            P("seq", "head"),
            P("head", None, None),
            P("seq", "head"),
            P("seq", "head"),
            P("seq", "head"),
            P("head", None, None, None),
            P("head", None),
            P("seq", "head"),
            P("seq", "head"),
            P("seq", "head"),
        ),
        out_specs=(P("seq", "head"), P("head", "seq", None, None)),
        check_vma=False,
    )
```

```python
import math

import jax
import jax.numpy as jnp
from jax import lax
from jax.experimental import pallas as pl
from jax.experimental.pallas import tpu as pltpu
from jax.sharding import PartitionSpec as P

MESH = pl.DeviceIdType.MESH
BF = jnp.bfloat16
F32 = jnp.float32
WIN = 512
HD = 128
GW = 256
FD = 512
RING = 8
HALF = 768
PIECE = GW // RING
PARTS = 4
SCALE2 = math.log2(math.e) / math.sqrt(HD)
INV = 1.0 / math.sqrt(FD)
LIMIT = math.sqrt(FD * FD) / 2.0
ORDER = (4, 3, 5, 2, 6, 1, 7)
LAST = (1, 7, 2, 6, 3, 5, 4)
VMEM_LIMIT = 66_700_000
NT = (((1,), (1,)), ((), ()))


def remote(src, dst, send, recv, peer):
    return pltpu.make_async_remote_copy(
        src_ref=src, dst_ref=dst, send_sem=send, recv_sem=recv, device_id=peer, device_id_type=MESH
    )


def rows(start, size):
    return pl.ds(pl.multiple_of(start, size), size)


def attend(query, kext, vext, out, start, count, first, last):
    span = count + 2 * WIN
    before, after = WIN - start, WIN + WIN - start
    row = lax.broadcasted_iota(jnp.int32, (count, 1), 0)
    low = jnp.maximum(row, jnp.where(first, before, 0))
    high = jnp.minimum(row + 2 * WIN, jnp.where(last, after - 1, span))
    col_b = lax.broadcasted_iota(jnp.int32, (count, before), 1)
    col_a = lax.broadcasted_iota(jnp.int32, (count, span - after), 1) + after
    keep_b, keep_a = col_b >= low, col_a <= high
    parts = []
    for head in range(GW // HD):
        lanes = slice(head * HD, (head + 1) * HD)
        scores = lax.dot_general(
            query[:, lanes], kext[start : start + span, lanes], NT, preferred_element_type=F32
        )
        s_b = jnp.where(keep_b, scores[:, :before], -jnp.inf)
        s_o = scores[:, before:after]
        s_a = jnp.where(keep_a, scores[:, after:], -jnp.inf)
        top = jnp.maximum(
            jnp.max(s_o, axis=1, keepdims=True),
            jnp.maximum(jnp.max(s_b, axis=1, keepdims=True), jnp.max(s_a, axis=1, keepdims=True)),
        )
        shift = top * SCALE2
        e_b, e_o, e_a = (jnp.exp2(s * SCALE2 - shift) for s in (s_b, s_o, s_a))
        total = (
            jnp.sum(e_b, axis=1, keepdims=True)
            + jnp.sum(e_o, axis=1, keepdims=True)
            + jnp.sum(e_a, axis=1, keepdims=True)
        )
        probs = jnp.concatenate([e_b.astype(BF), e_o.astype(BF), e_a.astype(BF)], axis=1)
        mixed = jnp.dot(probs, vext[start : start + span, lanes], preferred_element_type=F32)
        parts.append(mixed / total)
    square = sum(jnp.sum(p * p, axis=1, keepdims=True) for p in parts)
    norm = lax.rsqrt(square * (1.0 / GW) + 1e-05)
    for head, part in enumerate(parts):
        out[:, head * HD : (head + 1) * HD] = (part * norm).astype(BF)


def kernel(
    q1_in, k1_in, v1_in, map_in, fk_in, fv_in, rates, w_in, omap_in, q2_in, k2_in, v2_in,
    out, rows_out,
    fk, fv, w, q1, fmap, k1, v1, normed, part_out, part_in, own, mine, got1, sum1, half1, got2, full,
    w_new, fq, omap, q2, k2, v2, product, direct, relay, joined_out, joined, two,
    load_sem, halo_send, halo_recv, pair_send, pair_recv,
    s1, r1, s2, r2, s3, r3, s4, r4, s5, r5, ds, dr, rs, rr, js, jr,
):
    seq, head = lax.axis_index("seq"), lax.axis_index("head")
    n_seq, n_head = lax.axis_size("seq"), lax.axis_size("head")
    core = lax.rem(seq, 2)
    y, z = seq // (2 * RING), lax.rem(seq // 2, RING)
    pos1 = jnp.where(core == 0, y, z)
    pos2 = jnp.where(core == 0, z, y)
    stride1 = jnp.where(core == 0, 2 * RING, 2)
    stride2 = jnp.where(core == 0, 2, 2 * RING)
    toward = jnp.where(core == 0, 1, n_head - 1)
    near = lax.rem(head + toward, n_head)
    back = lax.rem(head + n_head - toward, n_head)
    far = lax.rem(head + 2, n_head)

    def ring1(place):
        return (seq + (place - pos1) * stride1, head)

    def ring2(place):
        return (seq + (place - pos2) * stride2, head)

    def ahead(position, step):
        return lax.rem(position + step, RING)

    partner = (seq + 1 - 2 * core, head)
    following = (lax.rem(seq + 1, n_seq), head)
    previous = (lax.rem(seq + n_seq - 1, n_seq), head)
    outer = (jnp.where(core == 0, previous[0], following[0]), head)
    first, last = seq == 0, seq == n_seq - 1

    sources = (
        (fk_in, fk),
        (w_in, w),
        (fv_in, fv),
        (k1_in, k1.at[WIN : 2 * WIN]),
        (v1_in, v1.at[WIN : 2 * WIN]),
        (q1_in, q1),
        (map_in, fmap),
        (omap_in, omap),
        (q2_in, q2),
        (k2_in, k2.at[WIN : 2 * WIN]),
        (v2_in, v2.at[WIN : 2 * WIN]),
    )
    loads = [pltpu.make_async_copy(a, b, load_sem.at[i]) for i, (a, b) in enumerate(sources)]
    for copy in loads:
        copy.start()

    barrier = pltpu.get_barrier_semaphore()
    for step in ORDER:
        pl.semaphore_signal(barrier, inc=1, device_id=ring1(ahead(pos1, step)), device_id_type=MESH)
        pl.semaphore_signal(barrier, inc=1, device_id=ring2(ahead(pos2, step)), device_id_type=MESH)
    for peer in (partner, outer, (seq, near), (seq, back)):
        pl.semaphore_signal(barrier, inc=1, device_id=peer, device_id_type=MESH)

    def halos(keys_in, values_in, keys, values, base):
        return [
            remote(src, dst, halo_send.at[base + i], halo_recv.at[base + i], peer)
            for i, (src, dst, peer) in enumerate(
                (
                    (keys_in, keys.at[0:WIN], following),
                    (keys_in, keys.at[2 * WIN :], previous),
                    (values_in, values.at[0:WIN], following),
                    (values_in, values.at[2 * WIN :], previous),
                )
            )
        ]

    halo1 = halos(k1_in, v1_in, k1, v1, 0)
    halo2 = halos(k2_in, v2_in, k2, v2, 4)
    pair = [
        remote(part_out.at[m], part_in.at[m], pair_send.at[m], pair_recv.at[m], partner)
        for m in range(3)
    ]

    def piece(m, place):
        return pl.ds(pl.multiple_of(m * GW + place * PIECE, PIECE), PIECE)

    def quarter(place):
        return (rows((place // 4) * 16, 16), rows(lax.rem(place, 4) * HD, HD))

    def scatter1(m, step):
        to, sem = ahead(pos1, step), m * RING + step
        return remote(
            mine.at[piece(m, to)], got1.at[m * 7 + step - 1], s1.at[sem], r1.at[sem], ring1(to)
        )

    def scatter2(m, step):
        to, sem = ahead(pos2, step), m * RING + step
        return remote(
            sum1.at[m].at[quarter(to)], got2.at[m * 7 + step - 1], s2.at[sem], r2.at[sem], ring2(to)
        )

    def gather2(m, step):
        sem = m * RING + step
        block = full.at[core].at[piece(m, pos1)].at[quarter(pos2)]
        return remote(block, block, s3.at[sem], r3.at[sem], ring2(ahead(pos2, step)))

    def gather1(m, step):
        sem = m * RING + step
        block = full.at[core].at[piece(m, pos1)]
        return remote(block, block, s4.at[sem], r4.at[sem], ring1(ahead(pos1, step)))

    def across(m, step, side, place):
        sem = m * RING + step
        block = full.at[side].at[piece(m, ahead(place, RING - step))]
        return remote(block, block, s5.at[sem], r5.at[sem], partner)

    def start_scatter1(m):
        pair[m].wait_recv()
        block = slice(m * GW, (m + 1) * GW)
        total = own[block] + part_in[m].astype(F32)
        own[block] = total
        mine[block] = total.astype(BF)
        for step in ORDER:
            scatter1(m, step).start()

    def start_scatter2(m):
        total = own[piece(m, pos1)]
        for step in LAST:
            scatter1(m, step).wait_recv()
        for step in LAST:
            total = total + got1[m * 7 + step - 1].astype(F32)
        sum1[m] = total.astype(BF)
        half1[m] = total
        for step in ORDER:
            scatter2(m, step).start()

    def start_gather2(m):
        total = half1.at[m][quarter(pos2)]
        for step in LAST:
            scatter2(m, step).wait_recv()
        for step in LAST:
            total = total + got2[m * 7 + step - 1].astype(F32)
        full.at[core].at[piece(m, pos1)].at[quarter(pos2)][...] = total.astype(BF)
        for step in ORDER:
            gather2(m, step).start()

    def start_gather1(m):
        for step in LAST:
            gather2(m, step).wait_recv()
        for step in ORDER:
            gather1(m, step).start()
        across(m, 0, core, pos1).start()

    def pass_across(m):
        for step in LAST:
            gather1(m, step).wait_recv()
            across(m, step, core, pos1).start()

    def squares(m):
        for step in range(RING):
            across(m, step, 1 - core, pos2).wait_recv()
        acc = jnp.zeros((8, FD), F32)
        for side in range(2):
            for i in range(4):
                block = full[side, m * GW + i * 64 : m * GW + (i + 1) * 64, :].astype(F32)
                block = block * block
                for j in range(8):
                    acc = acc + block[j * 8 : (j + 1) * 8]
        return acc

    rate = rates[...]

    def forward(which):
        block = rows(which * GW, GW)
        gate = lax.dot_general(w[0, block, :], fk[...], NT, preferred_element_type=F32) * INV
        up = lax.dot_general(w[1, block, :], fk[...], NT, preferred_element_type=F32) * INV
        sigmoid = 1.0 / (1.0 + jnp.exp(-gate))
        silu = gate * sigmoid
        hidden = (rate * silu * up).astype(BF)
        slope = up * sigmoid * (1.0 + gate * (1.0 - sigmoid)) * INV
        return hidden, silu * INV, slope

    def backward(which):
        block = rows(which * GW, GW)
        return rate * lax.dot_general(w[2, block, :], fv[...], NT, preferred_element_type=F32)

    def send_part(m, value):
        part_out[m] = value.astype(BF)
        pair[m].start()

    for copy in loads[:2]:
        copy.wait()
    hidden_p, silu_p, slope_p = forward(1 - core)
    loads[2].wait()
    value = jnp.dot(hidden_p, fv[...], preferred_element_type=F32)
    pl.semaphore_wait(barrier, 2 * (RING - 1) + 4)
    for copy in halo1:
        copy.start()
    send_part(2, value)
    hidden_o, silu_o, slope_o = forward(core)
    own[2 * GW : 3 * GW] = jnp.dot(hidden_o, fv[...], preferred_element_type=F32)
    back_p = backward(1 - core)
    send_part(1, jnp.dot((back_p * silu_p).astype(BF), fk[...], preferred_element_type=F32))
    start_scatter1(2)
    send_part(0, jnp.dot((back_p * slope_p).astype(BF), fk[...], preferred_element_type=F32))
    back_o = backward(core)
    own[GW : 2 * GW] = jnp.dot(
        (back_o * silu_o).astype(BF), fk[...], preferred_element_type=F32
    )
    start_scatter1(1)
    own[0:GW] = jnp.dot((back_o * slope_o).astype(BF), fk[...], preferred_element_type=F32)
    start_scatter1(0)

    start_scatter2(2)
    start_scatter2(1)
    for copy in loads[3:7]:
        copy.wait()
    for copy in halo1:
        copy.wait_recv()

    def attend_first(start):
        block = slice(start, start + GW)
        attend(q1.at[block], k1, v1, normed.at[block], start, GW, first, last)

    attend_first(0)
    start_scatter2(0)
    start_gather2(2)
    start_gather2(1)
    start_gather1(2)
    start_gather1(1)
    start_gather2(0)
    attend_first(GW)
    fq[...] = jnp.dot(normed[...], fmap[...], preferred_element_type=F32).astype(BF)
    pass_across(2)
    start_gather1(0)
    pass_across(1)
    acc = squares(2)
    pass_across(0)
    for copy in halo2:
        copy.start()
    acc = acc + squares(1)
    acc = acc + squares(0)
    energy = jnp.sum(jnp.sum(acc, axis=0, keepdims=True), axis=1, keepdims=True)
    factor = jnp.minimum(1.0, LIMIT * lax.rsqrt(energy + 1e-06))

    for m in range(3):

        def renew(r, carry, m=m):
            old = w[m, rows(r * 64, 64), :].astype(F32)
            start = pl.multiple_of(m * GW + lax.rem(r, 4) * 64, 64)
            grad = full[r // 4, pl.ds(start, 64), :].astype(F32)
            stepped = old + factor * grad
            norm = jnp.sqrt(jnp.sum(old * old, axis=1, keepdims=True))
            scale = norm * lax.rsqrt(jnp.sum(stepped * stepped, axis=1, keepdims=True) + 1e-06)
            w_new[m, rows(r * 64, 64), :] = (stepped * scale).astype(BF)
            return carry

        lax.fori_loop(0, 8, renew, 0, unroll=4)

    size = WIN // PARTS

    def columns(group):
        return rows(group * GW, GW)

    def to_relay(i):
        block = slice(i * size, (i + 1) * size)
        return remote(
            product.at[block, columns(far)], relay.at[i], rs.at[i], rr.at[i], (seq, near)
        )

    def to_back(i):
        block = slice(i * size, (i + 1) * size)
        return remote(
            product.at[block, columns(back)], direct.at[i], ds.at[i], dr.at[i], (seq, back)
        )

    def to_near(i):
        return remote(joined_out.at[i], joined.at[i], js.at[i], jr.at[i], (seq, near))

    for copy in loads[7:]:
        copy.wait()
    for start in (0, GW):
        block = slice(start, start + GW)
        query = fq[block]
        gate = lax.dot_general(query, w_new[0], NT, preferred_element_type=F32) * INV
        up = lax.dot_general(query, w_new[1], NT, preferred_element_type=F32) * INV
        hidden = (gate / (1.0 + jnp.exp(-gate)) * up).astype(BF)
        raw = jnp.dot(hidden, w_new[2], preferred_element_type=F32)
        mean = jnp.sum(raw * raw, axis=1, keepdims=True) * (1.0 / FD)
        fast = (raw * lax.rsqrt(mean + 1e-05)).astype(BF)
        product[block] = jnp.dot(fast, omap[...], preferred_element_type=F32).astype(BF)
        for i in range(start // size, (start + GW) // size):
            to_relay(i).start()
            to_back(i).start()

    share = FD // n_seq
    low = lax.rem(seq * share, 16)
    for m in range(3):
        wide = w_new[m, rows((seq * share) // 16 * 16, 16), :].astype(F32)
        value = wide[0:share]
        for k in range(1, 16 // share):
            value = jnp.where(low == k * share, wide[k * share : (k + 1) * share], value)
        rows_out[m] = value.astype(BF)

    for i in range(PARTS):
        to_relay(i).wait_recv()
        block = slice(i * size, (i + 1) * size)
        value = product[block, columns(near)].astype(F32) + relay[i].astype(F32)
        joined_out[i] = value.astype(BF)
        to_near(i).start()

    for copy in halo2:
        copy.wait_recv()
    for i in range(PARTS):
        block = slice(i * size, (i + 1) * size)
        to_back(i).wait_recv()
        to_near(i).wait_recv()
        mixed = (
            product[block, columns(head)].astype(F32)
            + direct[i].astype(F32)
            + joined[i].astype(F32)
        )
        two[block] = (q2[block].astype(F32) + mixed).astype(BF)
        attend(two.at[block], k2, v2, out.at[block], i * size, size, first, last)

    for copy in halo1 + halo2 + pair:
        copy.wait_send()
    for m in range(3):
        for step in ORDER:
            scatter1(m, step).wait_send()
            scatter2(m, step).wait_send()
            gather2(m, step).wait_send()
            gather1(m, step).wait_send()
        for step in range(RING):
            across(m, step, core, pos1).wait_send()
    for i in range(PARTS):
        to_relay(i).wait_send()
        to_back(i).wait_send()
        to_near(i).wait_send()


def local(
    queries_first,
    keys_first,
    values_first,
    input_map,
    fast_keys,
    fast_values,
    step_rates,
    fast_weights,
    output_map,
    queries_second,
    keys_second,
    values_second,
):
    hbm = pl.BlockSpec(memory_space=pltpu.HBM)
    vmem = pl.BlockSpec(memory_space=pltpu.VMEM)
    dma = pltpu.SemaphoreType.DMA
    share = FD // lax.axis_size("seq")
    block_output, own_rows = pl.pallas_call(
        kernel,
        out_shape=(
            jax.ShapeDtypeStruct((WIN, GW), BF),
            jax.ShapeDtypeStruct((3, share, FD), BF),
        ),
        in_specs=[hbm] * 6 + [vmem] + [hbm] * 5,
        out_specs=(vmem, vmem),
        scratch_shapes=[
            pltpu.VMEM((WIN, FD), BF),
            pltpu.VMEM((WIN, FD), BF),
            pltpu.VMEM((3, FD, FD), BF),
            pltpu.VMEM((WIN, GW), BF),
            pltpu.VMEM((GW, FD), BF),
            pltpu.VMEM((3 * WIN, GW), BF),
            pltpu.VMEM((3 * WIN, GW), BF),
            pltpu.VMEM((WIN, GW), BF),
            pltpu.VMEM((3, GW, FD), BF),
            pltpu.VMEM((3, GW, FD), BF),
            pltpu.VMEM((HALF, FD), F32),
            pltpu.VMEM((HALF, FD), BF),
            pltpu.VMEM((3 * (RING - 1), PIECE, FD), BF),
            pltpu.VMEM((3, PIECE, FD), BF),
            pltpu.VMEM((3, PIECE, FD), F32),
            pltpu.VMEM((3 * (RING - 1), 16, HD), BF),
            pltpu.VMEM((2, HALF, FD), BF),
            pltpu.VMEM((3, FD, FD), BF),
            pltpu.VMEM((WIN, FD), BF),
            pltpu.VMEM((FD, 4 * GW), BF),
            pltpu.VMEM((WIN, GW), BF),
            pltpu.VMEM((3 * WIN, GW), BF),
            pltpu.VMEM((3 * WIN, GW), BF),
            pltpu.VMEM((WIN, 4 * GW), BF),
            pltpu.VMEM((PARTS, WIN // PARTS, GW), BF),
            pltpu.VMEM((PARTS, WIN // PARTS, GW), BF),
            pltpu.VMEM((PARTS, WIN // PARTS, GW), BF),
            pltpu.VMEM((PARTS, WIN // PARTS, GW), BF),
            pltpu.VMEM((WIN, GW), BF),
            dma((11,)),
            dma((8,)),
            dma((8,)),
            dma((3,)),
            dma((3,)),
        ]
        + [dma((3 * RING,))] * 10
        + [dma((PARTS,))] * 6,
        compiler_params=pltpu.CompilerParams(
            collective_id=0, has_side_effects=True, vmem_limit_bytes=VMEM_LIMIT
        ),
        name="stretch",
    )(
        queries_first,
        keys_first,
        values_first,
        input_map[0],
        fast_keys,
        fast_values,
        step_rates.reshape(1, WIN),
        jnp.transpose(fast_weights[0], (1, 0, 2)),
        output_map,
        queries_second,
        keys_second,
        values_second,
    )
    return (block_output, jnp.transpose(own_rows, (1, 0, 2))[None])


def solution(mesh):
    return jax.shard_map(
        local,
        mesh=mesh,
        in_specs=(
            P("seq", "head"),
            P("seq", "head"),
            P("seq", "head"),
            P("head", None, None),
            P("seq", "head"),
            P("seq", "head"),
            P("seq", "head"),
            P("head", None, None, None),
            P("head", None),
            P("seq", "head"),
            P("seq", "head"),
            P("seq", "head"),
        ),
        out_specs=(P("seq", "head"), P("head", "seq", None, None)),
        check_vma=False,
    )
```

```python
import math

import jax
import jax.numpy as jnp
from jax import lax
from jax.experimental import pallas as pl
from jax.experimental.pallas import tpu as pltpu
from jax.sharding import PartitionSpec as P

MESH = pl.DeviceIdType.MESH
BF = jnp.bfloat16
F32 = jnp.float32
WIN = 512
HD = 128
GW = 256
FD = 512
RING = 8
HALF = 768
PIECE = GW // RING
PARTS = 4
SCALE2 = math.log2(math.e) / math.sqrt(HD)
INV = 1.0 / math.sqrt(FD)
LIMIT = math.sqrt(FD * FD) / 2.0
ORDER = (4, 3, 5, 2, 6, 1, 7)
LAST = (1, 7, 2, 6, 3, 5, 4)
HALFP = 16
VMEM_LIMIT = 40 << 20
NT = (((1,), (1,)), ((), ()))


def remote(src, dst, send, recv, peer):
    return pltpu.make_async_remote_copy(
        src_ref=src, dst_ref=dst, send_sem=send, recv_sem=recv, device_id=peer, device_id_type=MESH
    )


def rows(start, size):
    return pl.ds(pl.multiple_of(start, size), size)


def attend(query, kext, vext, out, start, count, first, last):
    span = count + 2 * WIN
    before, after = WIN - start, WIN + WIN - start
    row = lax.broadcasted_iota(jnp.int32, (count, 1), 0)
    low = jnp.maximum(row, jnp.where(first, before, 0))
    high = jnp.minimum(row + 2 * WIN, jnp.where(last, after - 1, span))
    col_b = lax.broadcasted_iota(jnp.int32, (count, before), 1)
    col_a = lax.broadcasted_iota(jnp.int32, (count, span - after), 1) + after
    keep_b, keep_a = col_b >= low, col_a <= high
    parts = []
    for head in range(GW // HD):
        lanes = slice(head * HD, (head + 1) * HD)
        scores = lax.dot_general(
            query[:, lanes], kext[start : start + span, lanes], NT, preferred_element_type=F32
        )
        s_b = jnp.where(keep_b, scores[:, :before], -jnp.inf)
        s_o = scores[:, before:after]
        s_a = jnp.where(keep_a, scores[:, after:], -jnp.inf)
        top = jnp.maximum(
            jnp.max(s_o, axis=1, keepdims=True),
            jnp.maximum(jnp.max(s_b, axis=1, keepdims=True), jnp.max(s_a, axis=1, keepdims=True)),
        )
        shift = top * SCALE2
        e_b, e_o, e_a = (jnp.exp2(s * SCALE2 - shift) for s in (s_b, s_o, s_a))
        total = (
            jnp.sum(e_b, axis=1, keepdims=True)
            + jnp.sum(e_o, axis=1, keepdims=True)
            + jnp.sum(e_a, axis=1, keepdims=True)
        )
        probs = jnp.concatenate([e_b.astype(BF), e_o.astype(BF), e_a.astype(BF)], axis=1)
        mixed = jnp.dot(probs, vext[start : start + span, lanes], preferred_element_type=F32)
        parts.append(mixed / total)
    square = sum(jnp.sum(p * p, axis=1, keepdims=True) for p in parts)
    norm = lax.rsqrt(square * (1.0 / GW) + 1e-05)
    for head, part in enumerate(parts):
        out[:, head * HD : (head + 1) * HD] = (part * norm).astype(BF)


def kernel(
    q1_in, k1_in, v1_in, map_in, fk_in, fv_in, rates_in, w_in, omap_in, q2_in, k2_in, v2_in,
    out, rows_out,
    fk, fv, rates, w, q1, fmap, k1, v1, normed, part_out, part_in, own, mine, got1, joint, sum1, half1, got2, full,
    w_new, fq, omap, q2, k2, v2, product, direct, relay, joined_out, joined, two,
    load_sem, halo_send, halo_recv, pair_send, pair_recv,
    s1, r1, s2, r2, s3, r3, s4, r4, s5, r5, ds, dr, rs, rr, js, jr,
):
    seq, head = lax.axis_index("seq"), lax.axis_index("head")
    n_seq, n_head = lax.axis_size("seq"), lax.axis_size("head")
    core = lax.rem(seq, 2)
    y, z = seq // (2 * RING), lax.rem(seq // 2, RING)
    pos1 = jnp.where(core == 0, y, z)
    pos2 = jnp.where(core == 0, z, y)
    stride1 = jnp.where(core == 0, 2 * RING, 2)
    stride2 = jnp.where(core == 0, 2, 2 * RING)
    toward = jnp.where(core == 0, 1, n_head - 1)
    near = lax.rem(head + toward, n_head)
    back = lax.rem(head + n_head - toward, n_head)
    far = lax.rem(head + 2, n_head)

    def ring1(place):
        return (seq + (place - pos1) * stride1, head)

    def ring2(place):
        return (seq + (place - pos2) * stride2, head)

    def ahead(position, step):
        return lax.rem(position + step, RING)

    partner = (seq + 1 - 2 * core, head)
    following = (lax.rem(seq + 1, n_seq), head)
    previous = (lax.rem(seq + n_seq - 1, n_seq), head)
    outer = (jnp.where(core == 0, previous[0], following[0]), head)
    first, last = seq == 0, seq == n_seq - 1

    sources = (
        (fk_in, fk),
        (w_in, w),
        (rates_in, rates),
        (fv_in, fv),
        (k1_in, k1.at[WIN : 2 * WIN]),
        (v1_in, v1.at[WIN : 2 * WIN]),
        (q1_in, q1),
        (map_in, fmap),
        (omap_in, omap),
        (q2_in, q2),
        (k2_in, k2.at[WIN : 2 * WIN]),
        (v2_in, v2.at[WIN : 2 * WIN]),
    )
    loads = [pltpu.make_async_copy(a, b, load_sem.at[i]) for i, (a, b) in enumerate(sources)]
    for copy in loads:
        copy.start()

    barrier = pltpu.get_barrier_semaphore()
    for step in (1, 2, 6, 7):
        pl.semaphore_signal(barrier, inc=1, device_id=ring1(ahead(pos1, step)), device_id_type=MESH)
    for step in ORDER:
        pl.semaphore_signal(barrier, inc=1, device_id=ring2(ahead(pos2, step)), device_id_type=MESH)
    for peer in (partner, outer, (seq, near), (seq, back)):
        pl.semaphore_signal(barrier, inc=1, device_id=peer, device_id_type=MESH)

    def halos(keys_in, values_in, keys, values, base):
        return [
            remote(src, dst, halo_send.at[base + i], halo_recv.at[base + i], peer)
            for i, (src, dst, peer) in enumerate(
                (
                    (keys_in, keys.at[0:WIN], following),
                    (keys_in, keys.at[2 * WIN :], previous),
                    (values_in, values.at[0:WIN], following),
                    (values_in, values.at[2 * WIN :], previous),
                )
            )
        ]

    halo1 = halos(k1_in, v1_in, k1, v1, 0)
    halo2 = halos(k2_in, v2_in, k2, v2, 4)
    pair = [
        remote(part_out.at[m], part_in.at[m], pair_send.at[m], pair_recv.at[m], partner)
        for m in range(3)
    ]

    def piece(m, place):
        return pl.ds(pl.multiple_of(m * GW + place * PIECE, PIECE), PIECE)

    def quarter(place):
        return (rows((place // 4) * 16, 16), rows(lax.rem(place, 4) * HD, HD))

    def part(m, place, half):
        start = m * GW + place * PIECE + half * HALFP
        return pl.ds(pl.multiple_of(start, HALFP), HALFP)

    def scatter1(m, step):
        sem, slot = m * RING + step, got1.at[m * 7 + (step or 4) - 1]
        to = ring1(ahead(pos1, {1: 1, 2: 2, 3: 1, 4: 2, 5: 7, 6: 6, 7: 7, 0: 6}[step]))
        if step in (2, 6):
            src = joint.at[m * 2 + step // 6]
        elif step in (4, 0):
            half = 0 if step == 4 else 1
            src = mine.at[part(m, ahead(pos1, 4), half)]
            slot = slot.at[half * HALFP : (half + 1) * HALFP]
        else:
            src = mine.at[piece(m, ahead(pos1, step))]
        return remote(src, slot, s1.at[sem], r1.at[sem], to)

    def scatter2(m, step):
        to, sem = ahead(pos2, step), m * RING + step
        return remote(
            sum1.at[m].at[quarter(to)], got2.at[m * 7 + step - 1], s2.at[sem], r2.at[sem], ring2(to)
        )

    def gather2(m, step):
        sem = m * RING + step
        block = full.at[core].at[piece(m, pos1)].at[quarter(pos2)]
        return remote(block, block, s3.at[sem], r3.at[sem], ring2(ahead(pos2, step)))

    def gather1(m, step):
        sem = m * RING + step
        to = ring1(ahead(pos1, {1: 1, 2: 2, 3: 1, 4: 2, 5: 7, 6: 6, 7: 7, 0: 6}[step]))
        behind, before = ahead(pos1, 6), ahead(pos1, 2)
        if step == 3:
            where = piece(m, behind)
        elif step == 5:
            where = piece(m, before)
        elif step == 4:
            where = part(m, behind, 0)
        elif step == 0:
            where = part(m, before, 1)
        else:
            where = piece(m, pos1)
        block = full.at[core].at[where]
        return remote(block, block, s4.at[sem], r4.at[sem], to)

    def across(m, step, side, place):
        sem = m * RING + step
        block = full.at[side].at[piece(m, ahead(place, RING - step))]
        return remote(block, block, s5.at[sem], r5.at[sem], partner)

    def start_scatter1(m):
        pair[m].wait_recv()
        block = slice(m * GW, (m + 1) * GW)
        total = own[block] + part_in[m].astype(F32)
        own[block] = total
        mine[block] = total.astype(BF)
        for step in (4, 0, 3, 5, 1, 7):
            scatter1(m, step).start()

    def join_scatter1(m):
        for side, (whole, half, step) in enumerate(((3, 4, 2), (5, 0, 6))):
            value = own[piece(m, ahead(pos1, step))]
            scatter1(m, whole).wait_recv()
            value = value + got1[m * 7 + whole - 1].astype(F32)
            scatter1(m, half).wait_recv()
            lines = slice(side * HALFP, (side + 1) * HALFP)
            extra = value[lines] + got1[m * 7 + 3, lines, :].astype(F32)
            other = value[HALFP - side * HALFP : PIECE - side * HALFP]
            joint[m * 2 + side, lines, :] = extra.astype(BF)
            joint[m * 2 + side, HALFP - side * HALFP : PIECE - side * HALFP, :] = other.astype(BF)
            scatter1(m, step).start()

    def start_scatter2(m):
        total = own[piece(m, pos1)]
        for step in (1, 7, 2, 6):
            scatter1(m, step).wait_recv()
        for step in (1, 7, 2, 6):
            total = total + got1[m * 7 + step - 1].astype(F32)
        sum1[m] = total.astype(BF)
        half1[m] = total
        for step in ORDER:
            scatter2(m, step).start()

    def start_gather2(m):
        total = half1.at[m][quarter(pos2)]
        for step in LAST:
            scatter2(m, step).wait_recv()
        for step in LAST:
            total = total + got2[m * 7 + step - 1].astype(F32)
        full.at[core].at[piece(m, pos1)].at[quarter(pos2)][...] = total.astype(BF)
        for step in ORDER:
            gather2(m, step).start()

    def start_gather1(m):
        for step in LAST:
            gather2(m, step).wait_recv()
        for step in (2, 6, 1, 7):
            gather1(m, step).start()
        across(m, 0, core, pos1).start()

    def forward_gather1(m):
        for step, onward in ((2, (3, 4)), (6, (5, 0))):
            gather1(m, step).wait_recv()
            for onto in onward:
                gather1(m, onto).start()
            across(m, step, core, pos1).start()

    def pass_across(m):
        for step in (1, 7, 3, 5, 4):
            gather1(m, step).wait_recv()
            if step == 4:
                gather1(m, 0).wait_recv()
            across(m, step, core, pos1).start()

    def squares(m):
        for step in range(RING):
            across(m, step, 1 - core, pos2).wait_recv()
        acc = jnp.zeros((8, FD), F32)
        for side in range(2):
            for i in range(4):
                block = full[side, m * GW + i * 64 : m * GW + (i + 1) * 64, :].astype(F32)
                block = block * block
                for j in range(8):
                    acc = acc + block[j * 8 : (j + 1) * 8]
        return acc

    def forward(which):
        block = rows(which * GW, GW)
        rate = rates[...]
        gate = lax.dot_general(w[0, block, :], fk[...], NT, preferred_element_type=F32) * INV
        up = lax.dot_general(w[1, block, :], fk[...], NT, preferred_element_type=F32) * INV
        sigmoid = 1.0 / (1.0 + jnp.exp(-gate))
        silu = gate * sigmoid
        hidden = (rate * silu * up).astype(BF)
        slope = up * sigmoid * (1.0 + gate * (1.0 - sigmoid)) * INV
        return hidden, silu * INV, slope

    def backward(which):
        block = rows(which * GW, GW)
        return rates[...] * lax.dot_general(w[2, block, :], fv[...], NT, preferred_element_type=F32)

    def send_part(m, value):
        part_out[m] = value.astype(BF)
        pair[m].start()

    for copy in loads[:3]:
        copy.wait()
    hidden_p, silu_p, slope_p = forward(1 - core)
    loads[3].wait()
    value = jnp.dot(hidden_p, fv[...], preferred_element_type=F32)
    pl.semaphore_wait(barrier, 4 + (RING - 1) + 4)
    for copy in halo1:
        copy.start()
    send_part(2, value)
    hidden_o, silu_o, slope_o = forward(core)
    own[2 * GW : 3 * GW] = jnp.dot(hidden_o, fv[...], preferred_element_type=F32)
    back_p = backward(1 - core)
    send_part(1, jnp.dot((back_p * silu_p).astype(BF), fk[...], preferred_element_type=F32))
    start_scatter1(2)
    send_part(0, jnp.dot((back_p * slope_p).astype(BF), fk[...], preferred_element_type=F32))
    back_o = backward(core)
    own[GW : 2 * GW] = jnp.dot(
        (back_o * silu_o).astype(BF), fk[...], preferred_element_type=F32
    )
    start_scatter1(1)
    own[0:GW] = jnp.dot((back_o * slope_o).astype(BF), fk[...], preferred_element_type=F32)
    start_scatter1(0)

    def attend_first(start):
        block = slice(start, start + GW)
        attend(q1.at[block], k1, v1, normed.at[block], start, GW, first, last)

    join_scatter1(2)
    join_scatter1(1)
    join_scatter1(0)
    start_scatter2(2)
    start_scatter2(1)
    start_scatter2(0)
    start_gather2(2)
    start_gather2(1)
    start_gather2(0)
    for copy in loads[4:8]:
        copy.wait()
    for copy in halo1:
        copy.wait_recv()
    attend_first(0)
    start_gather1(2)
    start_gather1(1)
    start_gather1(0)
    attend_first(GW)
    fq[...] = jnp.dot(normed[...], fmap[...], preferred_element_type=F32).astype(BF)
    forward_gather1(2)
    forward_gather1(1)
    forward_gather1(0)
    pass_across(2)
    pass_across(1)
    acc = squares(2)
    pass_across(0)
    acc = acc + squares(1)
    acc = acc + squares(0)
    for copy in halo2:
        copy.start()
    energy = jnp.sum(jnp.sum(acc, axis=0, keepdims=True), axis=1, keepdims=True)
    factor = jnp.minimum(1.0, LIMIT * lax.rsqrt(energy + 1e-06))

    for m in range(3):

        def renew(r, carry, m=m):
            old = w[m, rows(r * 64, 64), :].astype(F32)
            start = pl.multiple_of(m * GW + lax.rem(r, 4) * 64, 64)
            grad = full[r // 4, pl.ds(start, 64), :].astype(F32)
            stepped = old + factor * grad
            norm = jnp.sqrt(jnp.sum(old * old, axis=1, keepdims=True))
            scale = norm * lax.rsqrt(jnp.sum(stepped * stepped, axis=1, keepdims=True) + 1e-06)
            w_new[m, rows(r * 64, 64), :] = (stepped * scale).astype(BF)
            return carry

        lax.fori_loop(0, 8, renew, 0, unroll=8)

    size = WIN // PARTS

    def columns(group):
        return rows(group * GW, GW)

    def to_relay(i):
        block = slice(i * size, (i + 1) * size)
        return remote(
            product.at[block, columns(far)], relay.at[i], rs.at[i], rr.at[i], (seq, near)
        )

    def to_back(i):
        block = slice(i * size, (i + 1) * size)
        return remote(
            product.at[block, columns(back)], direct.at[i], ds.at[i], dr.at[i], (seq, back)
        )

    def to_near(i):
        return remote(joined_out.at[i], joined.at[i], js.at[i], jr.at[i], (seq, near))

    for copy in loads[8:]:
        copy.wait()
    for start in (0, GW):
        block = slice(start, start + GW)
        query = fq[block]
        gate = lax.dot_general(query, w_new[0], NT, preferred_element_type=F32) * INV
        up = lax.dot_general(query, w_new[1], NT, preferred_element_type=F32) * INV
        hidden = (gate / (1.0 + jnp.exp(-gate)) * up).astype(BF)
        raw = jnp.dot(hidden, w_new[2], preferred_element_type=F32)
        mean = jnp.sum(raw * raw, axis=1, keepdims=True) * (1.0 / FD)
        fast = (raw * lax.rsqrt(mean + 1e-05)).astype(BF)
        product[block] = jnp.dot(fast, omap[...], preferred_element_type=F32).astype(BF)
        for i in range(start // size, (start + GW) // size):
            to_relay(i).start()
            to_back(i).start()

    share = FD // n_seq
    low = lax.rem(seq * share, 16)
    for m in range(3):
        wide = w_new[m, rows((seq * share) // 16 * 16, 16), :].astype(F32)
        value = wide[0:share]
        for k in range(1, 16 // share):
            value = jnp.where(low == k * share, wide[k * share : (k + 1) * share], value)
        rows_out[m] = value.astype(BF)

    for i in range(PARTS):
        to_relay(i).wait_recv()
        block = slice(i * size, (i + 1) * size)
        value = product[block, columns(near)].astype(F32) + relay[i].astype(F32)
        joined_out[i] = value.astype(BF)
        to_near(i).start()

    for copy in halo2:
        copy.wait_recv()
    for i in range(PARTS):
        block = slice(i * size, (i + 1) * size)
        to_back(i).wait_recv()
        to_near(i).wait_recv()
        mixed = (
            product[block, columns(head)].astype(F32)
            + direct[i].astype(F32)
            + joined[i].astype(F32)
        )
        two[block] = (q2[block].astype(F32) + mixed).astype(BF)
        attend(two.at[block], k2, v2, out.at[block], i * size, size, first, last)

    for copy in halo1 + halo2 + pair:
        copy.wait_send()
    for m in range(3):
        for step in ORDER:
            scatter2(m, step).wait_send()
            gather2(m, step).wait_send()
        for step in range(RING):
            scatter1(m, step).wait_send()
            gather1(m, step).wait_send()
            across(m, step, core, pos1).wait_send()
    for i in range(PARTS):
        to_relay(i).wait_send()
        to_back(i).wait_send()
        to_near(i).wait_send()


def local(
    queries_first,
    keys_first,
    values_first,
    input_map,
    fast_keys,
    fast_values,
    step_rates,
    fast_weights,
    output_map,
    queries_second,
    keys_second,
    values_second,
):
    hbm = pl.BlockSpec(memory_space=pltpu.HBM)
    vmem = pl.BlockSpec(memory_space=pltpu.VMEM)
    dma = pltpu.SemaphoreType.DMA
    share = FD // lax.axis_size("seq")
    block_output, own_rows = pl.pallas_call(
        kernel,
        out_shape=(
            jax.ShapeDtypeStruct((WIN, GW), BF),
            jax.ShapeDtypeStruct((3, share, FD), BF),
        ),
        in_specs=[hbm] * 12,
        out_specs=(vmem, vmem),
        scratch_shapes=[
            pltpu.VMEM((WIN, FD), BF),
            pltpu.VMEM((WIN, FD), BF),
            pltpu.VMEM((1, WIN), F32),
            pltpu.VMEM((3, FD, FD), BF),
            pltpu.VMEM((WIN, GW), BF),
            pltpu.VMEM((GW, FD), BF),
            pltpu.VMEM((3 * WIN, GW), BF),
            pltpu.VMEM((3 * WIN, GW), BF),
            pltpu.VMEM((WIN, GW), BF),
            pltpu.VMEM((3, GW, FD), BF),
            pltpu.VMEM((3, GW, FD), BF),
            pltpu.VMEM((HALF, FD), F32),
            pltpu.VMEM((HALF, FD), BF),
            pltpu.VMEM((3 * (RING - 1), PIECE, FD), BF),
            pltpu.VMEM((6, PIECE, FD), BF),
            pltpu.VMEM((3, PIECE, FD), BF),
            pltpu.VMEM((3, PIECE, FD), F32),
            pltpu.VMEM((3 * (RING - 1), 16, HD), BF),
            pltpu.VMEM((2, HALF, FD), BF),
            pltpu.VMEM((3, FD, FD), BF),
            pltpu.VMEM((WIN, FD), BF),
            pltpu.VMEM((FD, 4 * GW), BF),
            pltpu.VMEM((WIN, GW), BF),
            pltpu.VMEM((3 * WIN, GW), BF),
            pltpu.VMEM((3 * WIN, GW), BF),
            pltpu.VMEM((WIN, 4 * GW), BF),
            pltpu.VMEM((PARTS, WIN // PARTS, GW), BF),
            pltpu.VMEM((PARTS, WIN // PARTS, GW), BF),
            pltpu.VMEM((PARTS, WIN // PARTS, GW), BF),
            pltpu.VMEM((PARTS, WIN // PARTS, GW), BF),
            pltpu.VMEM((WIN, GW), BF),
            dma((12,)),
            dma((8,)),
            dma((8,)),
            dma((3,)),
            dma((3,)),
        ]
        + [dma((3 * RING,))] * 10
        + [dma((PARTS,))] * 6,
        compiler_params=pltpu.CompilerParams(
            collective_id=0, has_side_effects=True, vmem_limit_bytes=VMEM_LIMIT
        ),
        name="stretch",
    )(
        *(
            pltpu.with_memory_space_constraint(x, pltpu.HBM)
            for x in (queries_first, keys_first, values_first, input_map[0], fast_keys, fast_values)
        ),
        pltpu.with_memory_space_constraint(step_rates.reshape(1, WIN), pltpu.HBM),
        *(
            pltpu.with_memory_space_constraint(x, pltpu.HBM)
            for x in (
                jnp.transpose(fast_weights[0], (1, 0, 2)),
                output_map,
                queries_second,
                keys_second,
                values_second,
            )
        ),
    )
    return (block_output, jnp.transpose(own_rows, (1, 0, 2))[None])


def solution(mesh):
    return jax.shard_map(
        local,
        mesh=mesh,
        in_specs=(
            P("seq", "head"),
            P("seq", "head"),
            P("seq", "head"),
            P("head", None, None),
            P("seq", "head"),
            P("seq", "head"),
            P("seq", "head"),
            P("head", None, None, None),
            P("head", None),
            P("seq", "head"),
            P("seq", "head"),
            P("seq", "head"),
        ),
        out_specs=(P("seq", "head"), P("head", "seq", None, None)),
        check_vma=False,
    )
```

```python
import math

import jax
import jax.numpy as jnp
from jax import lax
from jax.experimental import pallas as pl
from jax.experimental.pallas import tpu as pltpu
from jax.sharding import PartitionSpec as P

MESH = pl.DeviceIdType.MESH
BF = jnp.bfloat16
F32 = jnp.float32
WIN = 512
HD = 128
GW = 256
FD = 512
RING = 8
HALF = 768
PIECE = GW // RING
PARTS = 4
SCALE2 = math.log2(math.e) / math.sqrt(HD)
INV = 1.0 / math.sqrt(FD)
LIMIT = math.sqrt(FD * FD) / 2.0
ORDER = (4, 3, 5, 2, 6, 1, 7)
LAST = (1, 7, 2, 6, 3, 5, 4)
HALFP = 16
VMEM_LIMIT = 40 << 20
NT = (((1,), (1,)), ((), ()))


def remote(src, dst, send, recv, peer):
    return pltpu.make_async_remote_copy(
        src_ref=src, dst_ref=dst, send_sem=send, recv_sem=recv, device_id=peer, device_id_type=MESH
    )


def rows(start, size):
    return pl.ds(pl.multiple_of(start, size), size)


def attend(query, kext, vext, out, start, count, first, last):
    span = count + 2 * WIN
    before, after = WIN - start, WIN + WIN - start
    row = lax.broadcasted_iota(jnp.int32, (count, 1), 0)
    low = jnp.maximum(row, jnp.where(first, before, 0))
    high = jnp.minimum(row + 2 * WIN, jnp.where(last, after - 1, span))
    col_b = lax.broadcasted_iota(jnp.int32, (count, before), 1)
    col_a = lax.broadcasted_iota(jnp.int32, (count, span - after), 1) + after
    keep_b, keep_a = col_b >= low, col_a <= high
    parts = []
    for head in range(GW // HD):
        lanes = slice(head * HD, (head + 1) * HD)
        scores = lax.dot_general(
            query[:, lanes], kext[start : start + span, lanes], NT, preferred_element_type=F32
        )
        s_b = jnp.where(keep_b, scores[:, :before], -jnp.inf)
        s_o = scores[:, before:after]
        s_a = jnp.where(keep_a, scores[:, after:], -jnp.inf)
        top = jnp.maximum(
            jnp.max(s_o, axis=1, keepdims=True),
            jnp.maximum(jnp.max(s_b, axis=1, keepdims=True), jnp.max(s_a, axis=1, keepdims=True)),
        )
        shift = top * SCALE2
        e_b, e_o, e_a = (jnp.exp2(s * SCALE2 - shift) for s in (s_b, s_o, s_a))
        total = (
            jnp.sum(e_b, axis=1, keepdims=True)
            + jnp.sum(e_o, axis=1, keepdims=True)
            + jnp.sum(e_a, axis=1, keepdims=True)
        )
        probs = jnp.concatenate([e_b.astype(BF), e_o.astype(BF), e_a.astype(BF)], axis=1)
        mixed = jnp.dot(probs, vext[start : start + span, lanes], preferred_element_type=F32)
        parts.append(mixed / total)
    square = sum(jnp.sum(p * p, axis=1, keepdims=True) for p in parts)
    norm = lax.rsqrt(square * (1.0 / GW) + 1e-05)
    for head, part in enumerate(parts):
        out[:, head * HD : (head + 1) * HD] = (part * norm).astype(BF)


def kernel(
    q1_in, k1_in, v1_in, map_in, fk_in, fv_in, rates_in, w_in, omap_in, q2_in, k2_in, v2_in,
    out, rows_out,
    fk, fv, rates, w, q1, fmap, k1, v1, normed, part_out, part_in, own, mine, got1, joint, sum1, half1, got2, full,
    w_new, fq, omap, q2, k2, v2, product, direct, relay, joined_out, joined, two, norms,
    load_sem, halo_send, halo_recv, pair_send, pair_recv,
    s1, r1, s2, r2, s3, r3, s4, r4, s5, r5, ds, dr, rs, rr, js, jr,
):
    seq, head = lax.axis_index("seq"), lax.axis_index("head")
    n_seq, n_head = lax.axis_size("seq"), lax.axis_size("head")
    core = lax.rem(seq, 2)
    y, z = seq // (2 * RING), lax.rem(seq // 2, RING)
    pos1 = jnp.where(core == 0, y, z)
    pos2 = jnp.where(core == 0, z, y)
    stride1 = jnp.where(core == 0, 2 * RING, 2)
    stride2 = jnp.where(core == 0, 2, 2 * RING)
    toward = jnp.where(core == 0, 1, n_head - 1)
    near = lax.rem(head + toward, n_head)
    back = lax.rem(head + n_head - toward, n_head)
    far = lax.rem(head + 2, n_head)

    def ring1(place):
        return (seq + (place - pos1) * stride1, head)

    def ring2(place):
        return (seq + (place - pos2) * stride2, head)

    def ahead(position, step):
        return lax.rem(position + step, RING)

    partner = (seq + 1 - 2 * core, head)
    following = (lax.rem(seq + 1, n_seq), head)
    previous = (lax.rem(seq + n_seq - 1, n_seq), head)
    outer = (jnp.where(core == 0, previous[0], following[0]), head)
    first, last = seq == 0, seq == n_seq - 1

    sources = (
        (fk_in, fk),
        (w_in, w),
        (rates_in, rates),
        (fv_in, fv),
        (k1_in, k1.at[WIN : 2 * WIN]),
        (v1_in, v1.at[WIN : 2 * WIN]),
        (q1_in, q1),
        (map_in, fmap),
        (omap_in, omap),
        (q2_in, q2),
        (k2_in, k2.at[WIN : 2 * WIN]),
        (v2_in, v2.at[WIN : 2 * WIN]),
    )
    loads = [pltpu.make_async_copy(a, b, load_sem.at[i]) for i, (a, b) in enumerate(sources)]
    for copy in loads:
        copy.start()

    barrier = pltpu.get_barrier_semaphore()
    for step in (1, 2, 6, 7):
        pl.semaphore_signal(barrier, inc=1, device_id=ring1(ahead(pos1, step)), device_id_type=MESH)
    for step in ORDER:
        pl.semaphore_signal(barrier, inc=1, device_id=ring2(ahead(pos2, step)), device_id_type=MESH)
    for peer in (partner, outer, (seq, near), (seq, back)):
        pl.semaphore_signal(barrier, inc=1, device_id=peer, device_id_type=MESH)

    def halos(keys_in, values_in, keys, values, base):
        return [
            remote(src, dst, halo_send.at[base + i], halo_recv.at[base + i], peer)
            for i, (src, dst, peer) in enumerate(
                (
                    (keys_in, keys.at[0:WIN], following),
                    (keys_in, keys.at[2 * WIN :], previous),
                    (values_in, values.at[0:WIN], following),
                    (values_in, values.at[2 * WIN :], previous),
                )
            )
        ]

    halo1 = halos(k1_in, v1_in, k1, v1, 0)
    halo2 = halos(k2_in, v2_in, k2, v2, 4)
    pair = [
        remote(part_out.at[m], part_in.at[m], pair_send.at[m], pair_recv.at[m], partner)
        for m in range(3)
    ]

    def piece(m, place):
        return pl.ds(pl.multiple_of(m * GW + place * PIECE, PIECE), PIECE)

    def quarter(place):
        return (rows((place // 4) * 16, 16), rows(lax.rem(place, 4) * HD, HD))

    def part(m, place, half):
        start = m * GW + place * PIECE + half * HALFP
        return pl.ds(pl.multiple_of(start, HALFP), HALFP)

    def scatter1(m, step):
        sem, slot = m * RING + step, got1.at[m * 7 + (step or 4) - 1]
        to = ring1(ahead(pos1, {1: 1, 2: 2, 3: 1, 4: 2, 5: 7, 6: 6, 7: 7, 0: 6}[step]))
        if step in (2, 6):
            src = joint.at[m * 2 + step // 6]
        elif step in (4, 0):
            half = 0 if step == 4 else 1
            src = mine.at[part(m, ahead(pos1, 4), half)]
            slot = slot.at[half * HALFP : (half + 1) * HALFP]
        else:
            src = mine.at[piece(m, ahead(pos1, step))]
        return remote(src, slot, s1.at[sem], r1.at[sem], to)

    def scatter2(m, step):
        to, sem = ahead(pos2, step), m * RING + step
        return remote(
            sum1.at[m].at[quarter(to)], got2.at[m * 7 + step - 1], s2.at[sem], r2.at[sem], ring2(to)
        )

    def gather2(m, step):
        sem = m * RING + step
        block = full.at[core].at[piece(m, pos1)].at[quarter(pos2)]
        return remote(block, block, s3.at[sem], r3.at[sem], ring2(ahead(pos2, step)))

    def gather1(m, step):
        sem = m * RING + step
        to = ring1(ahead(pos1, {1: 1, 2: 2, 3: 1, 4: 2, 5: 7, 6: 6, 7: 7, 0: 6}[step]))
        behind, before = ahead(pos1, 6), ahead(pos1, 2)
        if step == 3:
            where = piece(m, behind)
        elif step == 5:
            where = piece(m, before)
        elif step == 4:
            where = part(m, behind, 0)
        elif step == 0:
            where = part(m, before, 1)
        else:
            where = piece(m, pos1)
        block = full.at[core].at[where]
        return remote(block, block, s4.at[sem], r4.at[sem], to)

    def across(m, step, side, place):
        sem = m * RING + step
        block = full.at[side].at[piece(m, ahead(place, RING - step))]
        return remote(block, block, s5.at[sem], r5.at[sem], partner)

    def start_scatter1(m):
        pair[m].wait_recv()
        block = slice(m * GW, (m + 1) * GW)
        total = own[block] + part_in[m].astype(F32)
        own[block] = total
        mine[block] = total.astype(BF)
        for step in (4, 0, 3, 5, 1, 7):
            scatter1(m, step).start()

    def join_scatter1(m):
        for side, (whole, half, step) in enumerate(((3, 4, 2), (5, 0, 6))):
            value = own[piece(m, ahead(pos1, step))]
            scatter1(m, whole).wait_recv()
            value = value + got1[m * 7 + whole - 1].astype(F32)
            scatter1(m, half).wait_recv()
            lines = slice(side * HALFP, (side + 1) * HALFP)
            extra = value[lines] + got1[m * 7 + 3, lines, :].astype(F32)
            other = value[HALFP - side * HALFP : PIECE - side * HALFP]
            joint[m * 2 + side, lines, :] = extra.astype(BF)
            joint[m * 2 + side, HALFP - side * HALFP : PIECE - side * HALFP, :] = other.astype(BF)
            scatter1(m, step).start()

    def start_scatter2(m):
        total = own[piece(m, pos1)]
        for step in (1, 7, 2, 6):
            scatter1(m, step).wait_recv()
        for step in (1, 7, 2, 6):
            total = total + got1[m * 7 + step - 1].astype(F32)
        sum1[m] = total.astype(BF)
        half1[m] = total
        for step in ORDER:
            scatter2(m, step).start()

    def start_gather2(m):
        total = half1.at[m][quarter(pos2)]
        for step in LAST:
            scatter2(m, step).wait_recv()
        for step in LAST:
            total = total + got2[m * 7 + step - 1].astype(F32)
        full.at[core].at[piece(m, pos1)].at[quarter(pos2)][...] = total.astype(BF)
        for step in ORDER:
            gather2(m, step).start()

    def start_gather1(m):
        for step in LAST:
            gather2(m, step).wait_recv()
        for step in (2, 6, 1, 7):
            gather1(m, step).start()
        across(m, 0, core, pos1).start()

    def forward_gather1(m):
        for step, onward in ((2, (3, 4)), (6, (5, 0))):
            gather1(m, step).wait_recv()
            for onto in onward:
                gather1(m, onto).start()
            across(m, step, core, pos1).start()

    def pass_across(m):
        for step in (1, 7, 3, 5, 4):
            gather1(m, step).wait_recv()
            if step == 4:
                gather1(m, 0).wait_recv()
            across(m, step, core, pos1).start()

    def squares(m):
        for step in range(RING):
            across(m, step, 1 - core, pos2).wait_recv()
        acc = jnp.zeros((8, FD), F32)
        for side in range(2):
            for i in range(4):
                block = full[side, m * GW + i * 64 : m * GW + (i + 1) * 64, :].astype(F32)
                block = block * block
                for j in range(8):
                    acc = acc + block[j * 8 : (j + 1) * 8]
        return acc

    def forward(which):
        block = rows(which * GW, GW)
        rate = rates[...]
        gate = lax.dot_general(w[0, block, :], fk[...], NT, preferred_element_type=F32) * INV
        up = lax.dot_general(w[1, block, :], fk[...], NT, preferred_element_type=F32) * INV
        sigmoid = 1.0 / (1.0 + jnp.exp(-gate))
        silu = gate * sigmoid
        hidden = (rate * silu * up).astype(BF)
        slope = up * sigmoid * (1.0 + gate * (1.0 - sigmoid)) * INV
        return hidden, silu * INV, slope

    def backward(which):
        block = rows(which * GW, GW)
        return rates[...] * lax.dot_general(w[2, block, :], fv[...], NT, preferred_element_type=F32)

    def send_part(m, value):
        part_out[m] = value.astype(BF)
        pair[m].start()

    for copy in loads[:3]:
        copy.wait()
    hidden_p, silu_p, slope_p = forward(1 - core)
    loads[3].wait()
    value = jnp.dot(hidden_p, fv[...], preferred_element_type=F32)
    pl.semaphore_wait(barrier, 4 + (RING - 1) + 4)
    for copy in halo1:
        copy.start()
    send_part(2, value)
    hidden_o, silu_o, slope_o = forward(core)
    own[2 * GW : 3 * GW] = jnp.dot(hidden_o, fv[...], preferred_element_type=F32)
    back_p = backward(1 - core)
    send_part(1, jnp.dot((back_p * silu_p).astype(BF), fk[...], preferred_element_type=F32))
    start_scatter1(2)
    send_part(0, jnp.dot((back_p * slope_p).astype(BF), fk[...], preferred_element_type=F32))
    back_o = backward(core)
    own[GW : 2 * GW] = jnp.dot(
        (back_o * silu_o).astype(BF), fk[...], preferred_element_type=F32
    )
    start_scatter1(1)
    own[0:GW] = jnp.dot((back_o * slope_o).astype(BF), fk[...], preferred_element_type=F32)
    start_scatter1(0)

    def attend_first(start):
        block = slice(start, start + GW)
        attend(q1.at[block], k1, v1, normed.at[block], start, GW, first, last)

    join_scatter1(2)
    join_scatter1(1)
    join_scatter1(0)
    start_scatter2(2)
    start_scatter2(1)
    start_scatter2(0)
    for copy in loads[4:8]:
        copy.wait()
    for copy in halo1:
        copy.wait_recv()
    attend_first(0)
    start_gather2(2)
    start_gather2(1)
    start_gather2(0)
    attend_first(GW)
    for m in range(3):
        old = w[m].astype(F32)
        norms[m * FD : (m + 1) * FD] = jnp.sqrt(jnp.sum(old * old, axis=1, keepdims=True))
    start_gather1(2)
    start_gather1(1)
    start_gather1(0)
    fq[...] = jnp.dot(normed[...], fmap[...], preferred_element_type=F32).astype(BF)
    forward_gather1(2)
    forward_gather1(1)
    forward_gather1(0)
    pass_across(2)
    pass_across(1)
    acc = squares(2)
    pass_across(0)
    acc = acc + squares(1)
    acc = acc + squares(0)
    for copy in halo2:
        copy.start()
    energy = jnp.sum(jnp.sum(acc, axis=0, keepdims=True), axis=1, keepdims=True)
    factor = jnp.minimum(1.0, LIMIT * lax.rsqrt(energy + 1e-06))

    for m in range(3):

        def renew(r, carry, m=m):
            old = w[m, rows(r * 64, 64), :].astype(F32)
            start = pl.multiple_of(m * GW + lax.rem(r, 4) * 64, 64)
            grad = full[r // 4, pl.ds(start, 64), :].astype(F32)
            stepped = old + factor * grad
            scale = norms[rows(m * FD + r * 64, 64), :] * lax.rsqrt(jnp.sum(stepped * stepped, axis=1, keepdims=True) + 1e-06)
            w_new[m, rows(r * 64, 64), :] = (stepped * scale).astype(BF)
            return carry

        lax.fori_loop(0, 8, renew, 0, unroll=8)

    size = WIN // PARTS

    def columns(group):
        return rows(group * GW, GW)

    def to_relay(i):
        block = slice(i * size, (i + 1) * size)
        return remote(
            product.at[block, columns(far)], relay.at[i], rs.at[i], rr.at[i], (seq, near)
        )

    def to_back(i):
        block = slice(i * size, (i + 1) * size)
        return remote(
            product.at[block, columns(back)], direct.at[i], ds.at[i], dr.at[i], (seq, back)
        )

    def to_near(i):
        return remote(joined_out.at[i], joined.at[i], js.at[i], jr.at[i], (seq, near))

    for copy in loads[8:]:
        copy.wait()
    for start in (0, GW):
        block = slice(start, start + GW)
        query = fq[block]
        gate = lax.dot_general(query, w_new[0], NT, preferred_element_type=F32) * INV
        up = lax.dot_general(query, w_new[1], NT, preferred_element_type=F32) * INV
        hidden = (gate / (1.0 + jnp.exp(-gate)) * up).astype(BF)
        raw = jnp.dot(hidden, w_new[2], preferred_element_type=F32)
        mean = jnp.sum(raw * raw, axis=1, keepdims=True) * (1.0 / FD)
        fast = (raw * lax.rsqrt(mean + 1e-05)).astype(BF)
        product[block] = jnp.dot(fast, omap[...], preferred_element_type=F32).astype(BF)
        for i in range(start // size, (start + GW) // size):
            to_relay(i).start()
            to_back(i).start()

    share = FD // n_seq
    low = lax.rem(seq * share, 16)
    for m in range(3):
        wide = w_new[m, rows((seq * share) // 16 * 16, 16), :].astype(F32)
        value = wide[0:share]
        for k in range(1, 16 // share):
            value = jnp.where(low == k * share, wide[k * share : (k + 1) * share], value)
        rows_out[m] = value.astype(BF)

    for i in range(PARTS):
        to_relay(i).wait_recv()
        block = slice(i * size, (i + 1) * size)
        value = product[block, columns(near)].astype(F32) + relay[i].astype(F32)
        joined_out[i] = value.astype(BF)
        to_near(i).start()

    for copy in halo2:
        copy.wait_recv()
    for i in range(PARTS):
        block = slice(i * size, (i + 1) * size)
        to_back(i).wait_recv()
        to_near(i).wait_recv()
        mixed = (
            product[block, columns(head)].astype(F32)
            + direct[i].astype(F32)
            + joined[i].astype(F32)
        )
        two[block] = (q2[block].astype(F32) + mixed).astype(BF)
        attend(two.at[block], k2, v2, out.at[block], i * size, size, first, last)

    for copy in halo1 + halo2 + pair:
        copy.wait_send()
    for m in range(3):
        for step in ORDER:
            scatter2(m, step).wait_send()
            gather2(m, step).wait_send()
        for step in range(RING):
            scatter1(m, step).wait_send()
            gather1(m, step).wait_send()
            across(m, step, core, pos1).wait_send()
    for i in range(PARTS):
        to_relay(i).wait_send()
        to_back(i).wait_send()
        to_near(i).wait_send()


def local(
    queries_first,
    keys_first,
    values_first,
    input_map,
    fast_keys,
    fast_values,
    step_rates,
    fast_weights,
    output_map,
    queries_second,
    keys_second,
    values_second,
):
    hbm = pl.BlockSpec(memory_space=pltpu.HBM)
    vmem = pl.BlockSpec(memory_space=pltpu.VMEM)
    dma = pltpu.SemaphoreType.DMA
    share = FD // lax.axis_size("seq")
    block_output, own_rows = pl.pallas_call(
        kernel,
        out_shape=(
            jax.ShapeDtypeStruct((WIN, GW), BF),
            jax.ShapeDtypeStruct((3, share, FD), BF),
        ),
        in_specs=[hbm] * 12,
        out_specs=(vmem, vmem),
        scratch_shapes=[
            pltpu.VMEM((WIN, FD), BF),
            pltpu.VMEM((WIN, FD), BF),
            pltpu.VMEM((1, WIN), F32),
            pltpu.VMEM((3, FD, FD), BF),
            pltpu.VMEM((WIN, GW), BF),
            pltpu.VMEM((GW, FD), BF),
            pltpu.VMEM((3 * WIN, GW), BF),
            pltpu.VMEM((3 * WIN, GW), BF),
            pltpu.VMEM((WIN, GW), BF),
            pltpu.VMEM((3, GW, FD), BF),
            pltpu.VMEM((3, GW, FD), BF),
            pltpu.VMEM((HALF, FD), F32),
            pltpu.VMEM((HALF, FD), BF),
            pltpu.VMEM((3 * (RING - 1), PIECE, FD), BF),
            pltpu.VMEM((6, PIECE, FD), BF),
            pltpu.VMEM((3, PIECE, FD), BF),
            pltpu.VMEM((3, PIECE, FD), F32),
            pltpu.VMEM((3 * (RING - 1), 16, HD), BF),
            pltpu.VMEM((2, HALF, FD), BF),
            pltpu.VMEM((3, FD, FD), BF),
            pltpu.VMEM((WIN, FD), BF),
            pltpu.VMEM((FD, 4 * GW), BF),
            pltpu.VMEM((WIN, GW), BF),
            pltpu.VMEM((3 * WIN, GW), BF),
            pltpu.VMEM((3 * WIN, GW), BF),
            pltpu.VMEM((WIN, 4 * GW), BF),
            pltpu.VMEM((PARTS, WIN // PARTS, GW), BF),
            pltpu.VMEM((PARTS, WIN // PARTS, GW), BF),
            pltpu.VMEM((PARTS, WIN // PARTS, GW), BF),
            pltpu.VMEM((PARTS, WIN // PARTS, GW), BF),
            pltpu.VMEM((WIN, GW), BF),
            pltpu.VMEM((3 * FD, 1), F32),
            dma((12,)),
            dma((8,)),
            dma((8,)),
            dma((3,)),
            dma((3,)),
        ]
        + [dma((3 * RING,))] * 10
        + [dma((PARTS,))] * 6,
        compiler_params=pltpu.CompilerParams(
            collective_id=0, has_side_effects=True, vmem_limit_bytes=VMEM_LIMIT
        ),
        name="stretch",
    )(
        *(
            pltpu.with_memory_space_constraint(x, pltpu.HBM)
            for x in (queries_first, keys_first, values_first, input_map[0], fast_keys, fast_values)
        ),
        pltpu.with_memory_space_constraint(step_rates.reshape(1, WIN), pltpu.HBM),
        *(
            pltpu.with_memory_space_constraint(x, pltpu.HBM)
            for x in (
                jnp.transpose(fast_weights[0], (1, 0, 2)),
                output_map,
                queries_second,
                keys_second,
                values_second,
            )
        ),
    )
    return (block_output, jnp.transpose(own_rows, (1, 0, 2))[None])


def solution(mesh):
    return jax.shard_map(
        local,
        mesh=mesh,
        in_specs=(
            P("seq", "head"),
            P("seq", "head"),
            P("seq", "head"),
            P("head", None, None),
            P("seq", "head"),
            P("seq", "head"),
            P("seq", "head"),
            P("head", None, None, None),
            P("head", None),
            P("seq", "head"),
            P("seq", "head"),
            P("seq", "head"),
        ),
        out_specs=(P("seq", "head"), P("head", "seq", None, None)),
        check_vma=False,
    )
```
